32 devices in a mesh: aa: 4 (over x, core), ba: 8 (over z, y).
Axes of the slice: x: 2, y: 2, z: 4, core: 2. Of those that a mesh axis runs over, the one named last changes fastest.
Arguments:
- positions: float32 [3, 16384], P(None, ('aa', 'ba')), may hold values from -1.5 to 1.5
- forces: float32 [3, 16384], P(None, ('aa', 'ba')), may hold values from -3 to 3
- tension: float32 [16384], P(('aa', 'ba')), may hold values from -6 to 6
- node_slot: int32 [16384], P(('aa', 'ba')), may hold values from 0 to 16383, as said below
- leaf_local: float32 [512, 3, 128], P(('aa', 'ba')), may hold values from -24 to 24
- parent_local: float32 [64, 3, 128], P(('aa', 'ba')), may hold values from -24 to 24
- l2l_maps: float32 [8, 384, 384], replicated, may hold values from -0.3125 to 0.3125
- leaf_parent: int32 [512], P(('aa', 'ba')), may hold values from 0 to 63, as said below
- leaf_octant: int32 [512], P(('aa', 'ba')), may hold values from 0 to 7
- near_list: int32 [512, 27], P(('aa', 'ba')), may hold values from 0 to 511, as said below
- blocks: float32 [256, 256, 256], P(('aa', 'ba')), may hold values from -0.375 to 0.375
Outputs:
- result: float32 [256, 256], P(('aa', 'ba'))
The draws below stay inside these ranges and needn't reach their ends.
Inputs may be any that keep to these rules, and one draw needn't show every extreme that they name: `node_slot`: A permutation. Of the nodes of one device (512 in a row), at most 64 have slots in the range of any one device (512 consecutive slots), and some pair of devices reaches 64. Every device has nodes in the ranges of the devices just before and just after it, counted round. `leaf_parent`: the parent of a leaf of device d lies among parents 2 * (d - 1) to 2 * (d + 2) - 1. `near_list`: each row holds 27 different leaves, the first the leaf itself, all within 128 leaves of it.
All inputs are finite; a program needn't handle non-finite values. Where the reference program divides by a largest or mean magnitude, that divisor is 1e-20 or more.
Results may differ from the reference program's by a relative error of at most 0.00012.
Values sent between devices are 32-bit elements; how exact they have to be, the bound alone decides.
A program may use at most 64 MiB of HBM per device.

```python
import jax
import jax.numpy as jnp
from jax import lax

NPF = 64
BLK = 256
NODE_DEV = 512
FIBERS = 256
NODES = 16384
LPTS = 32
LEAF_DEV = 16
LEAVES = 512
PAR_DEV = 2
PARENTS = 64
NEQ = 128
NEAR = 27
REACH = 8
MOST = 4
PIECE = 16


def draw_node_slot(key, part):
    devices = NODES // NODE_DEV
    groups = devices // MOST
    bins_drawn = jax.random.randint(jax.random.fold_in(key, 11), (groups, MOST), 0, MOST)
    bins_drawn = bins_drawn.at[0].set(0)
    bins_drawn = bins_drawn.at[1].set(jnp.arange(MOST))
    counts = jnp.sum((bins_drawn[:, :, None] == jnp.arange(MOST)[None, None, :]).astype(jnp.int32), axis=1).reshape(-1)
    values = jnp.arange(devices)
    pinned = (values == devices // 2) | (values == 1) | (values == devices - 1)
    score = jax.random.permutation(jax.random.fold_in(key, 12), devices) + devices * pinned.astype(jnp.int32)
    remaining = jnp.argsort(score, stable=True)[:devices - 3]
    other_spots = jnp.array([spot for spot in range(devices) if spot not in (0, MOST, MOST + 1)], jnp.int32)
    shuffled = jnp.zeros((devices,), jnp.int32).at[other_spots].set(remaining.astype(jnp.int32))
    shuffled = shuffled.at[jnp.array([0, MOST, MOST + 1], jnp.int32)].set(jnp.array([devices // 2, 1, devices - 1], jnp.int32))
    by_offset = jnp.zeros((devices,), jnp.int32).at[shuffled].set(counts)
    cumulative = jnp.cumsum(by_offset)
    offset_of = jnp.searchsorted(cumulative, jnp.arange(devices), side='right').astype(jnp.int32)

    def shuffle_one(subkey):
        return jax.random.permutation(subkey, devices)
    send_order = jax.vmap(shuffle_one)(jax.random.split(jax.random.fold_in(key, 13), devices))
    recv_order = jax.vmap(shuffle_one)(jax.random.split(jax.random.fold_in(key, 14), devices))
    source = jnp.arange(devices)[:, None]
    target = (source + offset_of[send_order]) % devices
    placed = recv_order[target, send_order]
    slot_ids = target[:, :, None] * NODE_DEV + placed[:, :, None] * PIECE + jnp.arange(PIECE)[None, None, :]
    return slot_ids.reshape(NODES).astype(jnp.int32)


def draw_leaf_parent(key, part):
    leaf_ids = jnp.arange(LEAVES)
    device = leaf_ids // LEAF_DEV
    inner = leaf_ids % LEAF_DEV
    first_parent = device * PAR_DEV + inner * PAR_DEV // LEAF_DEV
    jitter = jax.random.randint(jax.random.fold_in(key, 21), (LEAVES,), -2, 3)
    return jnp.clip(first_parent + jitter, 0, PARENTS - 1).astype(jnp.int32)


def draw_near_list(key, part):
    span = REACH * LEAF_DEV

    def pick_one(subkey):
        return jax.random.permutation(subkey, span)[:NEAR - 1] + 1
    distance = jax.vmap(pick_one)(jax.random.split(jax.random.fold_in(key, 31), LEAVES))
    direction = 2 * jax.random.randint(jax.random.fold_in(key, 32), (LEAVES, NEAR - 1), 0, 2) - 1
    leaf_ids = jnp.arange(LEAVES)[:, None]
    forward = leaf_ids + direction * distance
    inside = (forward >= 0) & (forward < LEAVES)
    chosen = jnp.where(inside, forward, leaf_ids - direction * distance)
    return jnp.concatenate([leaf_ids, chosen], axis=1).astype(jnp.int32)


def touch_ends(drawn, own_key, least, largest):
    shape = drawn.shape
    place = [jax.random.randint(jax.random.fold_in(own_key, axis), (), 0, shape[axis]) for axis in range(len(shape))]
    drawn = drawn.at[tuple(place)].set(least)
    longest = shape.index(max(shape))
    place[longest] = (place[longest] + 1) % shape[longest]
    return drawn.at[tuple(place)].set(largest)


def block_scale(own_key, shape, cuts, least, high):
    level, own = 1.0, jax.random.fold_in(own_key, 6)
    for dim, blocks in cuts:
        steps = jnp.exp(jax.random.uniform(jax.random.fold_in(own, dim), (blocks,), jnp.float32, least / len(cuts), high / len(cuts)))
        level = level * jnp.repeat(steps, shape[dim] // blocks).reshape([-1 if axis == dim else 1 for axis in range(len(shape))])
    return level


def bell_draw(key, shape, width, bound, cuts=(), held_as=jnp.bfloat16):
    values = jax.random.normal(key, shape, jnp.float32) * width
    if len(cuts) > 0:
        values = block_scale(key, shape, cuts, -0.22, 0.18) * values
    return jnp.clip(values, min=-bound, max=bound).astype(held_as)


def setup_inputs(seed: int = 0) -> dict:
    streams_of = jax.random.split(jax.random.key(seed), 12)
    return {
        "positions": bell_draw(streams_of[0], (3, NODES), 0.25, 1.5, ((1, 32),), jnp.float32),
        "forces": bell_draw(streams_of[1], (3, NODES), 0.5, 3.0, ((1, 32),), jnp.float32),
        "tension": bell_draw(streams_of[2], (NODES,), 1.0, 6.0, ((0, 32),), jnp.float32),
        "node_slot": draw_node_slot(jax.random.fold_in(streams_of[11], 71), 0),
        "leaf_local": bell_draw(streams_of[4], (LEAVES, 3, NEQ), 4.0, 24.0, ((0, 32),), jnp.float32),
        "parent_local": bell_draw(streams_of[5], (PARENTS, 3, NEQ), 4.0, 24.0, ((0, 32),), jnp.float32),
        "l2l_maps": bell_draw(streams_of[6], (8, 3 * NEQ, 3 * NEQ), (3 * NEQ) ** -0.5, 0.3125, (), jnp.float32),
        "leaf_parent": draw_leaf_parent(jax.random.fold_in(streams_of[11], 71), 0),
        "leaf_octant": touch_ends(jax.random.randint(streams_of[8], (LEAVES,), 0, 8), jax.random.fold_in(streams_of[8], 1), 0, 7).astype(jnp.int32),
        "near_list": draw_near_list(jax.random.fold_in(streams_of[11], 71), 0),
        "blocks": bell_draw(streams_of[10], (FIBERS, BLK, BLK), BLK ** -0.5, 0.375, ((0, 32),), jnp.float32),
    }


exact_products = lax.Precision.HIGHEST
softening = 0.05
box_margin = 0.05
shell_radius = 2.95
golden_angle = 2.399963229728653
eight_pi = 25.132741228718345
leaf_group = 16

def surface(amount):
    indices = jnp.arange(amount).astype(jnp.float32) + 0.5
    height = 1.0 - 2.0 * indices / amount
    radius = jnp.sqrt(jnp.maximum(1.0 - height * height, 0.0))
    azimuth = indices * golden_angle
    spread = jnp.stack([radius * jnp.cos(azimuth), radius * jnp.sin(azimuth), height])
    return spread / lax.optimization_barrier(jnp.max(jnp.abs(spread), axis=0, keepdims=True))

def leaf_velocity(targets, sources, density, shell_points):
    center = lax.optimization_barrier(jnp.mean(targets, axis=2, keepdims=True))
    half_width = lax.optimization_barrier(jnp.max(jnp.abs(targets - center), axis=(1, 2), keepdims=True)) + box_margin
    equivalent = center + shell_radius * half_width * shell_points[None, :, :]
    separation = targets[:, :, :, None] - equivalent[:, :, None, :]
    inverse = 1.0 / jnp.sqrt(lax.optimization_barrier(jnp.sum(separation * separation, axis=1)))
    along = jnp.einsum('bkpq,bkq->bpq', separation, density, precision=exact_products)
    far_field = jnp.einsum('bpq,bkq->bkp', inverse, density, precision=exact_products)
    far_field = far_field + jnp.einsum('bkpq,bpq->bkp', separation, along * inverse ** 3, precision=exact_products)
    near_gap = targets[:, :, :, None] - sources[:, 0:3, None, :]
    distance_sq = lax.optimization_barrier(jnp.sum(near_gap * near_gap, axis=1))
    weight = (distance_sq + softening ** 2) ** (-1.5)
    strengths = sources[:, 3:6]
    projection = jnp.einsum('bkps,bks->bps', near_gap, strengths, precision=exact_products)
    near_field = jnp.einsum('bps,bks->bkp', (distance_sq + 2.0 * softening ** 2) * weight, strengths, precision=exact_products)
    near_field = near_field + jnp.einsum('bkps,bps->bkp', near_gap, projection * weight, precision=exact_products)
    return (far_field + near_field) / eight_pi

def reference(positions, forces, tension, node_slot, leaf_local, parent_local, l2l_maps, leaf_parent, leaf_octant, near_list, blocks):
    payload = jnp.concatenate([positions, forces], axis=0)
    tree_data = jnp.zeros((6, NODES), jnp.float32).at[:, node_slot].set(payload)
    leaf_data = tree_data.reshape(6, LEAVES, LPTS).transpose(1, 0, 2)
    flat_parent = parent_local[leaf_parent].reshape(LEAVES, 3 * NEQ)
    translated = jnp.zeros((LEAVES, 3 * NEQ), jnp.float32)
    for octant in range(8):
        image = jnp.dot(flat_parent, l2l_maps[octant].T, precision=exact_products)
        translated = jnp.where((leaf_octant == octant)[:, None], image, translated)
    density = leaf_local + translated.reshape(LEAVES, 3, NEQ)
    shell_points = surface(NEQ)
    groups = LEAVES // leaf_group

    def one_group(items):
        targets, near_rows, dens = items
        sources = leaf_data[near_rows].transpose(0, 2, 1, 3).reshape(leaf_group, 6, NEAR * LPTS)
        return leaf_velocity(targets, sources, dens, shell_points)
    velocity = lax.map(one_group, (leaf_data[:, 0:3].reshape(groups, leaf_group, 3, LPTS), near_list.reshape(groups, leaf_group, NEAR), density.reshape(groups, leaf_group, 3, NEQ)))
    velocity = velocity.reshape(LEAVES, 3, LPTS).transpose(1, 0, 2).reshape(3, NODES)
    fiber_velocity = velocity[:, node_slot]
    stacked = fiber_velocity.reshape(3, FIBERS, NPF).transpose(1, 0, 2).reshape(FIBERS, 3 * NPF)
    vector = jnp.concatenate([stacked, tension.reshape(FIBERS, NPF)], axis=1)
    return jnp.einsum('fij,fj->fi', blocks, vector, precision=exact_products)
```

```python
import functools

import jax
import jax.numpy as jnp
import numpy as np
from jax import lax
from jax.experimental import pallas as pl
from jax.experimental.pallas import tpu as pltpu
from jax.sharding import PartitionSpec as P

MOST = 4
NEAR_SPAN = 128

softening = 0.05
box_margin = 0.05
shell_radius = 2.95
golden_angle = 2.399963229728653
eight_pi = 25.132741228718345
LANES = 128
MESH = pl.DeviceIdType.MESH
f32, bf16, i32 = jnp.float32, jnp.bfloat16, jnp.int32


def surface(amount):
    indices = np.arange(amount, dtype=np.float32) + np.float32(0.5)
    height = np.float32(1.0) - np.float32(2.0) * indices / np.float32(amount)
    radius = np.sqrt(np.maximum(np.float32(1.0) - height * height, np.float32(0.0)))
    azimuth = indices * np.float32(golden_angle)
    spread = np.stack([radius * np.cos(azimuth), radius * np.sin(azimuth), height])
    return jnp.asarray(spread / np.max(np.abs(spread), axis=0, keepdims=True))


def split3(x):
    high = x.astype(bf16).astype(f32)
    rest = x - high
    middle = rest.astype(bf16).astype(f32)
    low = rest - middle
    return jnp.concatenate([high, middle, low], axis=0).astype(bf16)


def joined(r):
    n = r.shape[0] // 3
    return r[0:n] + (r[n : 2 * n] + r[2 * n : 3 * n])


def dot_t(a, b):
    return lax.dot_general(a, b, (((1,), (1,)), ((), ())), preferred_element_type=f32)


def dot_n(a, b):
    return lax.dot_general(a, b, (((1,), (0,)), ((), ())), preferred_element_type=f32)


def lane_sums(x):
    ones = jnp.ones((8, x.shape[1]), bf16)
    high = x.astype(bf16)
    rest = x - high.astype(f32)
    return dot_t(ones, high) + dot_t(ones, rest.astype(bf16))


def body(
    dims,
    fetches,
    pos_ref,
    frc_ref,
    ten_ref,
    slot_ref,
    lloc_ref,
    par_ref,
    lpar_ref,
    loct_ref,
    near_ref,
    shell_ref,
    maps_hbm,
    out_ref,
    maps_v,
    m1,
    m2,
    stage,
    stage2,
    send,
    recv,
    mine,
    wide,
    rep,
    tcol,
    parw,
    trans,
    dens,
    acc,
    rsend,
    rrecv,
    local_sem,
    a_send,
    a_recv,
    p_send,
    p_recv,
    h_send,
    h_recv,
    r_send,
    r_recv,
):
    major, minor, reach = dims
    D = major * minor
    nodes = slot_ref.shape[1]
    cap = MOST * (nodes // D)
    per = LANES // cap
    tiles = D * cap // LANES
    slots = D * cap
    leaves = lloc_ref.shape[1]
    points = nodes // leaves
    node_tiles = nodes // LANES
    in_tile = LANES // points
    near_count = near_ref.shape[1]
    n_par = par_ref.shape[1]
    me = lax.axis_index("aa") * minor + lax.axis_index("ba")

    def dev(t):
        return (lax.div(t, minor), lax.rem(t, minor))

    maps_copy = pltpu.make_async_copy(maps_hbm, maps_v, local_sem.at[0])
    barrier = pltpu.get_barrier_semaphore()
    for fetch in fetches:
        fetch.start()

    @pl.loop(1, D)
    def _(k):
        pl.semaphore_signal(
            barrier, inc=1, device_id=dev(lax.rem(me + k, D)), device_id_type=MESH
        )

    maps_copy.start()
    for fetch in fetches:
        fetch.wait()

    slot_f = slot_ref[...].astype(f32)
    owner = jnp.floor((slot_f + 0.5) * (1.0 / nodes))
    within = slot_f - owner * nodes
    stage[0:3, :] = pos_ref[...]
    stage[3:6, :] = frc_ref[...]
    stage[6:7, :] = within + 1.0
    stage[7:8, :] = jnp.zeros((1, nodes), f32)
    ids = lax.broadcasted_iota(i32, (D, nodes), 0).astype(f32)
    owns = jnp.where(ids == owner, 1.0, 0.0).astype(f32)
    before = jnp.where(
        lax.broadcasted_iota(i32, (nodes, nodes), 0)
        < lax.broadcasted_iota(i32, (nodes, nodes), 1),
        1.0,
        0.0,
    ).astype(bf16)
    counts = dot_n(owns.astype(bf16), before)
    rank = jnp.sum(owns * counts, axis=0, keepdims=True)
    place = (owner * cap + rank).astype(i32)
    payload = split3(stage[...])
    chunk = 2 * LANES
    folded = per == 2
    half_lanes = lax.broadcasted_iota(i32, (4, LANES), 1) < cap

    @pl.loop(0, slots // chunk)
    def _(c):
        rows = lax.broadcasted_iota(i32, (chunk, nodes), 0) + c * chunk
        hot = jnp.where(rows == place, 1.0, 0.0).astype(bf16)
        m1[pl.ds(pl.multiple_of(c * chunk, chunk), chunk), :] = hot
        packed = joined(dot_t(payload, hot))
        for h in range(2):
            tile = packed[:, h * LANES : (h + 1) * LANES]
            if folded:
                top, bottom = tile[0:4], tile[4:8]
                to = per * (2 * c + h)
                send[to] = jnp.where(half_lanes, top, pltpu.roll(bottom, cap, 1))
                send[to + 1] = jnp.where(half_lanes, pltpu.roll(top, cap, 1), bottom)
            else:
                send[2 * c + h] = tile

    pl.semaphore_wait(barrier, D - 1)

    def par_copy(step):
        return pltpu.make_async_remote_copy(
            src_ref=par_ref,
            dst_ref=parw.at[1 - step],
            send_sem=p_send.at[1 - step],
            recv_sem=p_recv.at[1 - step],
            device_id=dev(lax.rem(me + D + step, D)),
            device_id_type=MESH,
        )

    par_copy(1).start()
    par_copy(-1).start()

    def a2a(src, dst, s_sem, r_sem, to, single=False):
        return pltpu.make_async_remote_copy(
            src_ref=src.at[to if single else lax.div(to, per)],
            dst_ref=dst.at[me],
            send_sem=s_sem.at[0],
            recv_sem=r_sem.at[0],
            device_id=dev(to),
            device_id_type=MESH,
        )

    def all_of(dst, s_sem, r_sem):
        whole = dst.at[pl.ds(0, D - 1)]
        return pltpu.make_async_remote_copy(
            src_ref=whole,
            dst_ref=whole,
            send_sem=s_sem.at[0],
            recv_sem=r_sem.at[0],
            device_id=dev(lax.rem(me + 1, D)),
            device_id_type=MESH,
        )

    @pl.loop(1, D)
    def _(k):
        a2a(send, recv, a_send, a_recv, lax.rem(me + k, D), folded).start()

    recv[me] = send[me if folded else me // per]

    parw[1] = par_ref[...]
    par_copy(1).wait()
    par_copy(-1).wait()
    square = (leaves, leaves)
    diagonal = lax.broadcasted_iota(i32, square, 0) == lax.broadcasted_iota(i32, square, 1)

    def column(row):
        return jnp.sum(jnp.where(diagonal, row.astype(f32), 0.0), axis=1, keepdims=True)

    wanted = column(lpar_ref[...] - (me - 1) * n_par)
    parts = []
    for c in range(3):
        total = jnp.zeros((leaves, LANES), f32)
        for j in range(3 * n_par):
            row = parw[j // n_par, c, j % n_par : j % n_par + 1, :]
            total = jnp.where(wanted == j, row, total)
        parts.append(total)
    flat = jnp.concatenate(parts, axis=1)
    high = flat.astype(bf16)
    low = (flat - high.astype(f32)).astype(bf16)
    both = jnp.concatenate([high, low], axis=0)
    octant = column(loct_ref[...])
    def collect(dst, into):
        group = lax.broadcasted_iota(i32, dst.shape[1:], 1) // cap
        own = me % per

        @pl.loop(0, tiles)
        def _(t):
            total = jnp.zeros(dst.shape[1:], f32)
            for g in range(per):
                moved = pltpu.roll(dst[t * per + g], ((g + per - own) * cap) % LANES, 1)
                total = jnp.where(group == g, moved, total)
            at = pl.ds(pl.multiple_of(t * LANES, LANES), LANES)
            into[0 : total.shape[0], at] = total

    all_of(recv, a_send, a_recv).wait_recv()

    if folded:
        for t in range(tiles):
            at = slice(t * LANES, (t + 1) * LANES)
            a, b = recv[2 * t], recv[2 * t + 1]
            stage2[0:4, at] = jnp.where(half_lanes, a, pltpu.roll(b, cap, 1))
            stage2[4:8, at] = jnp.where(half_lanes, pltpu.roll(a, cap, 1), b)
    else:
        collect(recv, stage2)
    arrived = split3(stage2[...])
    where_to = stage2[6:7, :]
    for c in range(nodes // chunk):
        rows = (lax.broadcasted_iota(i32, (chunk, slots), 0) + (c * chunk + 1)).astype(f32)
        hot = jnp.where(rows == where_to, 1.0, 0.0).astype(bf16)
        m2[c * chunk : (c + 1) * chunk, :] = hot
        placed = joined(dot_t(arrived, hot))
        for h in range(2):
            t = 2 * c + h
            tile = placed[:, h * LANES : (h + 1) * LANES]
            for r in range(6):
                mine[r * node_tiles + t : r * node_tiles + t + 1, :] = tile[r : r + 1]
            tcol[t * LANES : (t + 1) * LANES, :] = jnp.transpose(tile)

    def halo(k, act):
        there = me - k if act == "wait_recv" else me + k

        @pl.when((there >= 0) & (there < D))
        def _():
            copy = pltpu.make_async_remote_copy(
                src_ref=mine,
                dst_ref=wide.at[reach - k],
                send_sem=h_send.at[reach - k],
                recv_sem=h_recv.at[reach - k],
                device_id=dev(there),
                device_id_type=MESH,
            )
            getattr(copy, act)()

    @pl.loop(0, reach)
    def _(j):
        halo(reach - j, "start")
        halo(j - reach, "start")

    wide[reach] = mine[...]

    maps_copy.wait()
    trans[...] = jnp.zeros(trans.shape, f32)

    @pl.loop(0, maps_v.shape[0])
    def _(o):
        m = maps_v[o]
        m_high = m.astype(bf16)
        m_low = (m - m_high.astype(f32)).astype(bf16)
        first = dot_t(both, m_high)
        image = first[0:leaves] + (first[leaves : 2 * leaves] + dot_t(high, m_low))
        trans[...] = jnp.where(octant == jnp.asarray(o, i32).astype(f32), image, trans[...])

    for c in range(3):
        dens[c] = lloc_ref[c] + trans[:, c * LANES : (c + 1) * LANES]

    def pair_sums(targets, gaps_from, strengths, eps2, sums):
        gap = [targets[c] - gaps_from[c] for c in range(3)]
        d2 = gap[0] * gap[0] + gap[1] * gap[1] + gap[2] * gap[2]
        soft = d2 + eps2 if eps2 else d2
        inverse = lax.rsqrt(soft)
        weight = inverse * inverse * inverse
        along = gap[0] * strengths[0] + gap[1] * strengths[1] + gap[2] * strengths[2]
        near = (soft + eps2) * weight if eps2 else inverse
        along = along * weight
        return [sums[c] + (near * strengths[c] + along * gap[c]) for c in range(3)]

    def targets_of(leaf):
        rows = tcol[pl.ds(pl.multiple_of(leaf * points, points), points), :]
        return [jnp.broadcast_to(rows[:, c : c + 1], (points, LANES)) for c in range(3)]

    @pl.loop(0, leaves)
    def _(leaf):
        targets = targets_of(leaf)
        center = [jnp.sum(x, axis=0, keepdims=True) * (1.0 / points) for x in targets]
        spread = [
            jnp.max(jnp.abs(targets[c] - center[c]), axis=0, keepdims=True) for c in range(3)
        ]
        half = jnp.maximum(jnp.maximum(spread[0], spread[1]), spread[2]) + box_margin
        points_at = [
            center[c] + shell_radius * half * shell_ref[c : c + 1, :] for c in range(3)
        ]
        density = [dens[c, pl.ds(leaf, 1), :] for c in range(3)]
        zero = jnp.zeros((points, LANES), f32)
        sums = pair_sums(targets, points_at, density, 0.0, [zero, zero, zero])
        for c in range(3):
            acc[c, pl.ds(pl.multiple_of(leaf * points, points), points), :] = sums[c]

    lane_group = lax.broadcasted_iota(i32, (8, LANES), 1) // points

    def spread_out(j):
        for t in range(node_tiles):
            rows = [wide[j, r * node_tiles + t : r * node_tiles + t + 1, :] for r in range(6)]
            tile = jnp.concatenate(rows + rows[0:2], axis=0)
            turned = [tile] + [pltpu.roll(tile, s * points, 1) for s in range(1, in_tile)]
            for i in range(in_tile):
                full = turned[(-i) % in_tile]
                for g in range(1, in_tile):
                    full = jnp.where(lane_group == g, turned[(g - i) % in_tile], full)
                rep[j * leaves + t * in_tile + i] = full

    spread_out(reach)

    @pl.loop(1, reach + 1)
    def _(k):
        halo(k, "wait_recv")
        spread_out(reach - k)
        halo(-k, "wait_recv")
        spread_out(reach + k)

    first_leaf = (me - reach) * leaves

    def table_row(leaf, n):
        row = near_ref[leaf, n] - first_leaf
        return jnp.minimum(jnp.maximum(row, 0), rep.shape[0] - 1)

    @pl.loop(0, leaves)
    def _(leaf):
        at = pl.ds(pl.multiple_of(leaf * points, points), points)
        targets = targets_of(leaf)
        sums = [acc[c, at, :] for c in range(3)]
        for base in range(0, near_count, in_tile):
            count = min(in_tile, near_count - base)
            source = rep[table_row(leaf, base)]
            for g in range(1, count):
                source = jnp.where(lane_group == g, rep[table_row(leaf, base + g)], source)
            if count < in_tile:
                row = lax.broadcasted_iota(i32, (8, LANES), 0)
                source = jnp.where((lane_group >= count) & (row >= 3), 0.0, source)
            sums = pair_sums(
                targets,
                [source[c : c + 1] for c in range(3)],
                [source[c + 3 : c + 4] for c in range(3)],
                softening**2,
                sums,
            )
        for c in range(3):
            acc[c, at, :] = sums[c]

    for c in range(3):
        stage[c : c + 1, :] = lane_sums(acc[c])[0:1] * (1.0 / eight_pi)
    velocity = split3(stage[...])

    @pl.loop(0, slots // chunk)
    def _(c):
        hot = m2[:, pl.ds(pl.multiple_of(c * chunk, chunk), chunk)]
        packed = joined(dot_n(velocity, hot))
        rsend[2 * c] = packed[0:4, 0:LANES]
        rsend[2 * c + 1] = packed[0:4, LANES:chunk]

    @pl.loop(1, D)
    def _(k):
        a2a(rsend, rrecv, r_send, r_recv, lax.rem(me + k, D)).start()

    rrecv[me] = rsend[me // per]

    all_of(recv, a_send, a_recv).wait_send()

    @pl.loop(1, reach + 1)
    def _(k):
        halo(k, "wait_send")
        halo(-k, "wait_send")


    all_of(rrecv, r_send, r_recv).wait_recv()

    collect(rrecv, stage2)
    stage2[4:8, :] = jnp.zeros((4, slots), f32)
    at_nodes = joined(dot_n(split3(stage2[...]), m1[...]))

    out_ref[...] = at_nodes
    all_of(rrecv, r_send, r_recv).wait_send()


def final(at_nodes, ten_ref, blocks_v, out_ref):
    fibers = blocks_v.shape[0]
    npf = at_nodes.shape[1] // fibers
    per_tile = LANES // npf
    left = lax.broadcasted_iota(i32, (1, LANES), 1) < npf
    for i in range(fibers):
        t, g = i // per_tile, i % per_tile
        lanes = slice(t * LANES, (t + 1) * LANES)
        x, y, z = (at_nodes[c : c + 1, lanes] for c in range(3))
        tension = ten_ref[0:1, lanes]

        def side(v, to):
            turn = ((to - g) * npf) % LANES
            return pltpu.roll(v, turn, 1) if turn else v

        first = jnp.where(left, side(x, 0), side(y, 1))
        second = jnp.where(left, side(z, 0), side(tension, 1))
        products = blocks_v[i, :, 0:LANES] * first + blocks_v[i, :, LANES : 2 * LANES] * second
        out_ref[i : i + 1, :] = lane_sums(products)[0:1]


def kernel(dims, count, *refs):
    given, held = refs[0:count], refs[count + 2 : 2 * count + 2]
    fetch_sem = refs[-1]
    fetches = [
        pltpu.make_async_copy(given[n], held[n], fetch_sem.at[n]) for n in range(count)
    ]
    body(dims, fetches, *held, *refs[count : count + 2], *refs[2 * count + 2 : -1])


def local(
    positions,
    forces,
    tension,
    node_slot,
    leaf_local,
    parent_local,
    l2l_maps,
    leaf_parent,
    leaf_octant,
    near_list,
    blocks,
):
    major, minor = lax.axis_size("aa"), lax.axis_size("ba")
    D = major * minor
    nodes = node_slot.shape[0]
    leaves, _, shell = leaf_local.shape
    reach = -(-NEAR_SPAN // leaves)
    cap = MOST * (nodes // D)
    slots = D * cap
    fibers, unknowns, _ = blocks.shape
    node_tiles = nodes // LANES
    folded = LANES == 2 * cap
    vmem = pl.BlockSpec(memory_space=pltpu.VMEM)
    anywhere = pl.BlockSpec(memory_space=pl.ANY)
    dma = pltpu.SemaphoreType.DMA
    operands = (
        positions,
        forces,
        tension.reshape(1, nodes),
        node_slot.reshape(1, nodes),
        leaf_local.transpose(1, 0, 2),
        parent_local.transpose(1, 0, 2),
        leaf_parent.reshape(1, leaves),
        leaf_octant.reshape(1, leaves),
        near_list,
        surface(shell),
    )
    held = [
        (pltpu.SMEM if x is near_list else pltpu.VMEM)(x.shape, x.dtype) for x in operands
    ]
    at_nodes = pl.pallas_call(
        functools.partial(kernel, (major, minor, reach), len(operands)),
        out_shape=pltpu.VMEM((8, nodes), f32),
        in_specs=[anywhere] * (len(operands) + 1),
        out_specs=vmem,
        scratch_shapes=held
        + [
            pltpu.VMEM(l2l_maps.shape, f32),
            pltpu.VMEM((slots, nodes), bf16),
            pltpu.VMEM((nodes, slots), bf16),
            pltpu.VMEM((8, nodes), f32),
            pltpu.VMEM((8, slots), f32),
            pltpu.VMEM((D, 4, LANES) if folded else (slots // LANES, 8, LANES), f32),
            pltpu.VMEM((D, 4 if folded else 8, LANES), f32),
            pltpu.VMEM((6 * node_tiles, LANES), f32),
            pltpu.VMEM((2 * reach + 1, 6 * node_tiles, LANES), f32),
            pltpu.VMEM(((2 * reach + 1) * leaves, 8, LANES), f32),
            pltpu.VMEM((nodes, 8), f32),
            pltpu.VMEM((3, 3, parent_local.shape[0], shell), f32),
            pltpu.VMEM((leaves, 3 * shell), f32),
            pltpu.VMEM((3, leaves, shell), f32),
            pltpu.VMEM((3, nodes, LANES), f32),
            pltpu.VMEM((slots // LANES, 4, LANES), f32),
            pltpu.VMEM((D, 4, LANES), f32),
            dma((2,)),
            dma((1,)),
            dma((1,)),
            dma((3,)),
            dma((3,)),
            dma((2 * reach + 1,)),
            dma((2 * reach + 1,)),
            dma((1,)),
            dma((1,)),
            dma((len(operands),)),
        ],
        compiler_params=pltpu.CompilerParams(
            collective_id=0, has_side_effects=True, vmem_limit_bytes=56 * 2**20
        ),
    )(*operands, l2l_maps)
    return pl.pallas_call(
        final,
        out_shape=jax.ShapeDtypeStruct((fibers, unknowns), f32),
        in_specs=[vmem, vmem, vmem],
        out_specs=vmem,
        compiler_params=pltpu.CompilerParams(vmem_limit_bytes=8*2**20),
    )(at_nodes, tension.reshape(1, nodes), blocks)


def solution(mesh):
    in_specs = (
        P(None, ("aa", "ba")),
        P(None, ("aa", "ba")),
        P(("aa", "ba")),
        P(("aa", "ba")),
        P(("aa", "ba"), None, None),
        P(("aa", "ba"), None, None),
        P(),
        P(("aa", "ba")),
        P(("aa", "ba")),
        P(("aa", "ba"), None),
        P(("aa", "ba"), None, None),
    )
    out_specs = P(("aa", "ba"), None)
    return jax.shard_map(local, mesh=mesh, in_specs=in_specs, out_specs=out_specs, check_vma=False)
```

```python
import functools

import jax
import jax.numpy as jnp
import numpy as np
from jax import lax
from jax.experimental import pallas as pl
from jax.experimental.pallas import tpu as pltpu
from jax.sharding import PartitionSpec as P

MOST = 4
NEAR_SPAN = 128

softening = 0.05
box_margin = 0.05
shell_radius = 2.95
golden_angle = 2.399963229728653
eight_pi = 25.132741228718345
LANES = 128
MESH = pl.DeviceIdType.MESH
f32, bf16, i32 = jnp.float32, jnp.bfloat16, jnp.int32


def surface(amount):
    indices = np.arange(amount, dtype=np.float32) + np.float32(0.5)
    height = np.float32(1.0) - np.float32(2.0) * indices / np.float32(amount)
    radius = np.sqrt(np.maximum(np.float32(1.0) - height * height, np.float32(0.0)))
    azimuth = indices * np.float32(golden_angle)
    spread = np.stack([radius * np.cos(azimuth), radius * np.sin(azimuth), height])
    return jnp.asarray(spread / np.max(np.abs(spread), axis=0, keepdims=True))


def split3_parts(x):
    high = x.astype(bf16).astype(f32)
    rest = x - high
    middle = rest.astype(bf16).astype(f32)
    return [high, middle, rest - middle]


def joined(r):
    n = r.shape[0] // 3
    return r[0:n] + (r[n : 2 * n] + r[2 * n : 3 * n])


def dot_t(a, b):
    return lax.dot_general(a, b, (((1,), (1,)), ((), ())), preferred_element_type=f32)


def dot_n(a, b):
    return lax.dot_general(a, b, (((1,), (0,)), ((), ())), preferred_element_type=f32)


def lane_sums(x):
    ones = jnp.ones((8, x.shape[1]), bf16)
    high = x.astype(bf16)
    rest = x - high.astype(f32)
    return dot_t(ones, high) + dot_t(ones, rest.astype(bf16))


def hot(condition):
    return jnp.where(condition, 1.0, 0.0).astype(bf16)


def body(
    dims,
    fetches,
    slot_ref,
    pos_ref,
    frc_ref,
    lloc_ref,
    par_ref,
    lpar_ref,
    loct_ref,
    near_ref,
    shell_ref,
    maps_hbm,
    out_ref,
    maps_v,
    rank_hot,
    lane_hot,
    stage,
    flat,
    send,
    recv,
    mine,
    wide,
    rep,
    spots,
    parw,
    trans,
    dens,
    acc,
    rsend,
    rrecv,
    local_sem,
    a_send,
    a_recv,
    p_send,
    p_recv,
    h_send,
    h_recv,
    r_send,
    r_recv,
):
    major, minor, reach = dims
    D = major * minor
    nodes = slot_ref.shape[1]
    cap = MOST * (nodes // D)
    per = LANES // cap
    tiles = D * cap // LANES
    slots = D * cap
    leaves = lloc_ref.shape[1]
    points = nodes // leaves
    node_tiles = nodes // LANES
    in_tile = LANES // points
    near_count = near_ref.shape[1]
    n_par = par_ref.shape[1]
    folds, rows_sent = send_form(cap)
    me = lax.axis_index("aa") * minor + lax.axis_index("ba")

    def dev(t):
        return (lax.div(t, minor), lax.rem(t, minor))

    maps_copy = pltpu.make_async_copy(maps_hbm, maps_v, local_sem.at[0])
    barrier = pltpu.get_barrier_semaphore()
    for fetch in fetches[0:3]:
        fetch.start()

    @pl.loop(1, D)
    def _(k):
        pl.semaphore_signal(
            barrier, inc=1, device_id=dev(lax.rem(me + k, D)), device_id_type=MESH
        )

    for fetch in fetches[3:]:
        fetch.start()
    maps_copy.start()
    for fetch in fetches[0:3]:
        fetch.wait()

    def owner_of(slot):
        return jnp.floor((slot + 0.5) * (1.0 / nodes))

    def rows_of(shape, group=1):
        row = lax.broadcasted_iota(i32, shape, 0)
        return (row // group if group > 1 else row).astype(f32)

    slot_f = slot_ref[...].astype(f32)
    owner = owner_of(slot_f)
    within = slot_f - owner * nodes
    tile_at = jnp.floor((within + 0.5) * (1.0 / LANES))
    stage[0:3, :] = pos_ref[...]
    stage[3:6, :] = frc_ref[...]
    stage[6:7, :] = within - tile_at * LANES + 1.0
    stage[7:8, :] = tile_at

    owns = jnp.where(rows_of((D, nodes)) == owner, 1.0, 0.0)
    by_tile = [owns[:, t * LANES : (t + 1) * LANES] for t in range(node_tiles)]
    square = (LANES, 2 * LANES)
    over = lax.broadcasted_iota(i32, square, 1)
    before = hot((lax.broadcasted_iota(i32, square, 0) < over) | (over >= LANES))
    counts = dot_n(jnp.concatenate(by_tile, axis=0).astype(bf16), before)
    ranks, base = [], jnp.zeros((D, LANES), f32)
    for t in range(node_tiles):
        at = slice(t * D, (t + 1) * D)
        ranks.append(
            jnp.sum(by_tile[t] * (counts[at, 0:LANES] + base), axis=0, keepdims=True)
        )
        base = base + counts[at, LANES : 2 * LANES]
    rank = jnp.concatenate(ranks, axis=1)
    lane_ids = rows_of((LANES, nodes))
    for g in range(per):
        rank_hot[g] = hot(lane_ids == rank + float(g * cap))

    pieces = split3_parts(stage[...])
    sent = D * rows_sent
    mask = hot(rows_of((sent, nodes), rows_sent) == owner)
    lhs = []
    for piece in pieces:
        folded = []
        for h in range(folds):
            rows = piece[h * rows_sent : (h + 1) * rows_sent]
            rows = jnp.concatenate([rows] * (16 // rows_sent), axis=0).astype(bf16)
            folded.append(
                jnp.concatenate(
                    [mask[b : b + 16] * rows for b in range(0, sent, 16)], axis=0
                )
            )
        lhs.append(jnp.concatenate(folded, axis=1) if folds > 1 else folded[0])
    places = [rank_hot[h] for h in range(folds)]
    packed = joined(
        dot_t(
            jnp.concatenate(lhs, axis=0),
            jnp.concatenate(places, axis=1) if folds > 1 else places[0],
        )
    )
    for o in range(D):
        send[o] = packed[o * rows_sent : (o + 1) * rows_sent]

    pl.semaphore_wait(barrier, D - 1)

    def a2a(src, dst, s_sem, r_sem, to, index):
        return pltpu.make_async_remote_copy(
            src_ref=src.at[index],
            dst_ref=dst.at[me],
            send_sem=s_sem.at[0],
            recv_sem=r_sem.at[0],
            device_id=dev(to),
            device_id_type=MESH,
        )

    def all_of(dst, s_sem, r_sem):
        whole = dst.at[pl.ds(0, D - 1)]
        return pltpu.make_async_remote_copy(
            src_ref=whole,
            dst_ref=whole,
            send_sem=s_sem.at[0],
            recv_sem=r_sem.at[0],
            device_id=dev(lax.rem(me + 1, D)),
            device_id_type=MESH,
        )

    @pl.loop(1, D)
    def _(k):
        to = lax.rem(me + k, D)
        a2a(send, recv, a_send, a_recv, to, to).start()

    def par_copy(step):
        return pltpu.make_async_remote_copy(
            src_ref=par_ref,
            dst_ref=parw.at[1 - step],
            send_sem=p_send.at[1 - step],
            recv_sem=p_recv.at[1 - step],
            device_id=dev(lax.rem(me + D + step, D)),
            device_id_type=MESH,
        )

    for fetch in fetches[3:]:
        fetch.wait()
    par_copy(1).start()
    par_copy(-1).start()
    recv[me] = send[me]
    parw[1] = par_ref[...]

    all_of(recv, a_send, a_recv).wait_recv()

    half_lanes = lax.broadcasted_iota(i32, (4, LANES), 1) < cap
    for t in range(tiles):
        at = slice(t * LANES, (t + 1) * LANES)
        if folds == 2:
            a, b = recv[2 * t], recv[2 * t + 1]
            flat[0:4, at] = jnp.where(half_lanes, a, pltpu.roll(b, cap, 1))
            flat[4:8, at] = jnp.where(half_lanes, pltpu.roll(a, cap, 1), b)
        else:
            total = recv[t * per]
            for g in range(1, per):
                total = total + pltpu.roll(recv[t * per + g], g * cap, 1)
            flat[:, at] = total
    arrived = split3_parts(flat[...])
    lane_row, tile_row = flat[6:7, :], flat[7:8, :]
    lane_hot[...] = hot(rows_of((LANES, slots)) + 1.0 == lane_row)
    masked = [
        jnp.where(tile_row == float(t), part, 0.0)
        for t in range(node_tiles)
        for part in arrived
    ]
    placed = dot_t(jnp.concatenate(masked, axis=0).astype(bf16), lane_hot[...])
    unit = jnp.where(
        lax.broadcasted_iota(i32, (8, LANES), 0) < 3, 1.0 / softening, 1.0
    )
    placed_tiles = [joined(placed[24 * t : 24 * t + 24]) * unit for t in range(node_tiles)]
    last = placed_tiles[-1]
    for t in range(node_tiles - 1):
        mine[8 * t : 8 * t + 6, :] = placed_tiles[t][0:6]
        mine[8 * t + 6 : 8 * t + 8, :] = last[2 * t : 2 * t + 2]

    def halo(k, act):
        there = me - k if act == "wait_recv" else me + k

        @pl.when((there >= 0) & (there < D))
        def _():
            copy = pltpu.make_async_remote_copy(
                src_ref=mine,
                dst_ref=wide.at[reach - k],
                send_sem=h_send.at[reach - k],
                recv_sem=h_recv.at[reach - k],
                device_id=dev(there),
                device_id_type=MESH,
            )
            getattr(copy, act)()

    @pl.loop(0, reach)
    def _(j):
        halo(reach - j, "start")
        halo(j - reach, "start")

    wide[reach] = mine[...]
    for t in range(node_tiles):
        turned = jnp.transpose(placed_tiles[t])
        at = slice(t * LANES, (t + 1) * LANES)
        for c in range(3):
            spots[c, at, :] = jnp.broadcast_to(turned[:, c : c + 1], (LANES, LANES))

    par_copy(1).wait()
    par_copy(-1).wait()
    diagonal_of = (leaves, leaves)
    diagonal = lax.broadcasted_iota(i32, diagonal_of, 0) == lax.broadcasted_iota(
        i32, diagonal_of, 1
    )

    def column(row):
        return jnp.sum(jnp.where(diagonal, row.astype(f32), 0.0), axis=1, keepdims=True)

    wanted = column(lpar_ref[...] - (me - 1) * n_par)
    parts = []
    for c in range(3):
        total = jnp.zeros((leaves, LANES), f32)
        for j in range(3 * n_par):
            row = parw[j // n_par, c, j % n_par : j % n_par + 1, :]
            total = jnp.where(wanted == j, row, total)
        parts.append(total)
    wide_row = jnp.concatenate(parts, axis=1)
    high = wide_row.astype(bf16)
    low = (wide_row - high.astype(f32)).astype(bf16)
    both = jnp.concatenate([high, low], axis=0)
    octant = column(loct_ref[...])

    maps_copy.wait()
    trans[...] = jnp.zeros(trans.shape, f32)

    @pl.loop(0, maps_v.shape[0])
    def _(o):
        m = maps_v[o]
        m_high = m.astype(bf16)
        m_low = (m - m_high.astype(f32)).astype(bf16)
        first = dot_t(both, m_high)
        image = first[0:leaves] + (first[leaves : 2 * leaves] + dot_t(high, m_low))
        trans[...] = jnp.where(octant == jnp.asarray(o, i32).astype(f32), image, trans[...])

    for c in range(3):
        dens[c] = lloc_ref[c] + trans[:, c * LANES : (c + 1) * LANES]

    def pair_sums(targets, gaps_from, strengths, soft_by, sums):
        gap = [targets[c] - gaps_from[c] for c in range(3)]
        d2 = gap[0] * gap[0] + gap[1] * gap[1] + gap[2] * gap[2]
        soft = d2 + 1.0 if soft_by else d2
        inverse = lax.rsqrt(soft)
        weight = inverse * inverse * inverse
        along = gap[0] * strengths[0] + gap[1] * strengths[1] + gap[2] * strengths[2]
        near = inverse + weight if soft_by else inverse
        along = along * weight
        return [sums[c] + (near * strengths[c] + along * gap[c]) for c in range(3)]

    def leaf_rows(leaf):
        return pl.ds(pl.multiple_of(leaf * points, points), points)

    @pl.loop(0, leaves)
    def _(leaf):
        at = leaf_rows(leaf)
        targets = [spots[c, at, :] for c in range(3)]
        center = [jnp.sum(x, axis=0, keepdims=True) * (1.0 / points) for x in targets]
        spread = [
            jnp.max(jnp.abs(targets[c] - center[c]), axis=0, keepdims=True) for c in range(3)
        ]
        half = jnp.maximum(jnp.maximum(spread[0], spread[1]), spread[2])
        half = half + box_margin / softening
        points_at = [
            center[c] + shell_radius * half * shell_ref[c : c + 1, :] for c in range(3)
        ]
        density = [dens[c, pl.ds(leaf, 1), :] for c in range(3)]
        zero = jnp.zeros((points, LANES), f32)
        sums = pair_sums(targets, points_at, density, False, [zero, zero, zero])
        for c in range(3):
            acc[c, at, :] = sums[c]

    lane_group = lax.broadcasted_iota(i32, (8, LANES), 1) // points

    def spread_out(j):
        for t in range(node_tiles):
            if t < node_tiles - 1:
                tile = wide[j, 8 * t : 8 * t + 8, :]
            else:
                ends = [wide[j, 8 * i + 6 : 8 * i + 8, :] for i in range(node_tiles - 1)]
                tile = jnp.concatenate(ends + ends[0:1], axis=0)
            turned = [tile] + [pltpu.roll(tile, s * points, 1) for s in range(1, in_tile)]
            for i in range(in_tile):
                full = turned[(-i) % in_tile]
                for g in range(1, in_tile):
                    full = jnp.where(lane_group == g, turned[(g - i) % in_tile], full)
                rep[j * leaves + t * in_tile + i] = full

    spread_out(reach)
    together = 2 if reach % 2 == 0 else 1

    @pl.loop(0, reach // together)
    def _(step):
        ks = [step * together + 1 + i for i in range(together)]
        for k in ks:
            halo(k, "wait_recv")
            halo(-k, "wait_recv")
        for k in ks:
            spread_out(reach - k)
            spread_out(reach + k)

    first_leaf = (me - reach) * leaves

    def table_row(leaf, n):
        row = near_ref[leaf, n] - first_leaf
        return jnp.minimum(jnp.maximum(row, 0), rep.shape[0] - 1)

    @pl.loop(0, leaves)
    def _(leaf):
        at = leaf_rows(leaf)
        targets = [spots[c, at, :] for c in range(3)]
        sums = [acc[c, at, :] for c in range(3)]
        for base in range(0, near_count, in_tile):
            count = min(in_tile, near_count - base)
            source = rep[table_row(leaf, base)]
            for g in range(1, count):
                source = jnp.where(lane_group == g, rep[table_row(leaf, base + g)], source)
            if count < in_tile:
                row = lax.broadcasted_iota(i32, (8, LANES), 0)
                source = jnp.where((lane_group >= count) & (row >= 3), 0.0, source)
            sums = pair_sums(
                targets,
                [source[c : c + 1] for c in range(3)],
                [source[c + 3 : c + 4] for c in range(3)],
                True,
                sums,
            )
        for c in range(3):
            acc[c, at, :] = sums[c]

    speed = [lane_sums(acc[c])[0:1] * (1.0 / (eight_pi * softening)) for c in range(3)]
    nothing = jnp.zeros((1, nodes), f32)
    coarse = [v.astype(bf16).astype(f32) for v in speed]
    eight = jnp.concatenate(
        coarse + [nothing] + [speed[c] - coarse[c] for c in range(3)] + [nothing], axis=0
    )
    rows = [eight[:, t * LANES : (t + 1) * LANES] for t in range(node_tiles)]
    moved = dot_n(jnp.concatenate(rows, axis=0).astype(bf16), lane_hot[...])
    tile_row = flat[7:8, :]
    back = moved[0:8]
    for t in range(1, node_tiles):
        back = jnp.where(tile_row == float(t), moved[8 * t : 8 * t + 8], back)
    back = back[0:4] + back[4:8]
    for t in range(tiles):
        rsend[t] = back[:, t * LANES : (t + 1) * LANES]

    @pl.loop(1, D)
    def _(k):
        to = lax.rem(me + k, D)
        a2a(rsend, rrecv, r_send, r_recv, to, lax.div(to, per)).start()

    rrecv[me] = rsend[me // per]

    all_of(recv, a_send, a_recv).wait_send()

    @pl.loop(1, reach + 1)
    def _(k):
        halo(k, "wait_send")
        halo(-k, "wait_send")

    all_of(rrecv, r_send, r_recv).wait_recv()

    got = jnp.concatenate([rrecv[o] for o in range(D)], axis=0)
    got_high = got.astype(bf16)
    got_low = (got - got_high.astype(f32)).astype(bf16)
    found = dot_n(jnp.concatenate([got_high, got_low], axis=0), rank_hot[me % per])
    owner = owner_of(slot_ref[...].astype(f32))
    pairs = rows_of((8, nodes), 4)
    total = jnp.zeros((8, nodes), f32)
    for b in range(D // 2):
        both_rows = found[8 * b : 8 * b + 8] + found[4 * D + 8 * b : 4 * D + 8 * b + 8]
        total = jnp.where(pairs + float(2 * b) == owner, both_rows, total)
    out_ref[...] = total[0:4] + total[4:8]

    all_of(rrecv, r_send, r_recv).wait_send()


def final(nodes_ref, ten_ref, blocks_v, out_ref):
    at_nodes = nodes_ref[...]
    fibers = blocks_v.shape[0]
    npf = at_nodes.shape[1] // fibers
    per_tile = LANES // npf
    left = lax.broadcasted_iota(i32, (1, LANES), 1) < npf
    for i in range(fibers):
        t, g = i // per_tile, i % per_tile
        lanes = slice(t * LANES, (t + 1) * LANES)
        x, y, z = (at_nodes[c : c + 1, lanes] for c in range(3))
        tension = ten_ref[0:1, lanes]

        def side(v, to):
            turn = ((to - g) * npf) % LANES
            return pltpu.roll(v, turn, 1) if turn else v

        first = jnp.where(left, side(x, 0), side(y, 1))
        second = jnp.where(left, side(z, 0), side(tension, 1))
        products = blocks_v[i, :, 0:LANES] * first + blocks_v[i, :, LANES : 2 * LANES] * second
        out_ref[i : i + 1, :] = lane_sums(products)[0:1]


def send_form(cap):
    folds = 2 if LANES == 2 * cap else 1
    return folds, 8 // folds


def kernel(dims, count, *refs):
    given, held = refs[0:count], refs[count + 2 : 2 * count + 2]
    fetch_sem = refs[-1]
    fetches = [
        pltpu.make_async_copy(given[n], held[n], fetch_sem.at[n]) for n in range(count)
    ]
    body(dims, fetches, *held, *refs[count : count + 2], *refs[2 * count + 2 : -1])


def local(
    positions,
    forces,
    tension,
    node_slot,
    leaf_local,
    parent_local,
    l2l_maps,
    leaf_parent,
    leaf_octant,
    near_list,
    blocks,
):
    major, minor = lax.axis_size("aa"), lax.axis_size("ba")
    D = major * minor
    nodes = node_slot.shape[0]
    leaves, _, shell = leaf_local.shape
    reach = -(-NEAR_SPAN // leaves)
    cap = MOST * (nodes // D)
    slots = D * cap
    fibers, unknowns, _ = blocks.shape
    node_tiles = nodes // LANES
    _, rows_sent = send_form(cap)
    vmem = pl.BlockSpec(memory_space=pltpu.VMEM)
    anywhere = pl.BlockSpec(memory_space=pl.ANY)
    dma = pltpu.SemaphoreType.DMA
    operands = (
        node_slot.reshape(1, nodes),
        positions,
        forces,
        leaf_local.transpose(1, 0, 2),
        parent_local.transpose(1, 0, 2),
        leaf_parent.reshape(1, leaves),
        leaf_octant.reshape(1, leaves),
        near_list,
        surface(shell),
    )
    held = [
        (pltpu.SMEM if x is near_list else pltpu.VMEM)(x.shape, x.dtype) for x in operands
    ]
    at_nodes = pl.pallas_call(
        functools.partial(kernel, (major, minor, reach), len(operands)),
        out_shape=pltpu.VMEM((4, nodes), f32),
        in_specs=[anywhere] * (len(operands) + 1),
        out_specs=vmem,
        scratch_shapes=held
        + [
            pltpu.VMEM(l2l_maps.shape, f32),
            pltpu.VMEM((LANES // cap, LANES, nodes), bf16),
            pltpu.VMEM((LANES, slots), bf16),
            pltpu.VMEM((8, nodes), f32),
            pltpu.VMEM((8, slots), f32),
            pltpu.VMEM((D, rows_sent, LANES), f32),
            pltpu.VMEM((D, rows_sent, LANES), f32),
            pltpu.VMEM((8 * (node_tiles - 1), LANES), f32),
            pltpu.VMEM((2 * reach + 1, 8 * (node_tiles - 1), LANES), f32),
            pltpu.VMEM(((2 * reach + 1) * leaves, 8, LANES), f32),
            pltpu.VMEM((3, nodes, LANES), f32),
            pltpu.VMEM((3, 3, parent_local.shape[0], shell), f32),
            pltpu.VMEM((leaves, 3 * shell), f32),
            pltpu.VMEM((3, leaves, shell), f32),
            pltpu.VMEM((3, nodes, LANES), f32),
            pltpu.VMEM((slots // LANES, 4, LANES), f32),
            pltpu.VMEM((D, 4, LANES), f32),
            dma((1,)),
            dma((1,)),
            dma((1,)),
            dma((3,)),
            dma((3,)),
            dma((2 * reach + 1,)),
            dma((2 * reach + 1,)),
            dma((1,)),
            dma((1,)),
            dma((len(operands),)),
        ],
        compiler_params=pltpu.CompilerParams(
            collective_id=0, has_side_effects=True, vmem_limit_bytes=56 * 2**20
        ),
    )(*operands, l2l_maps)
    return pl.pallas_call(
        final,
        out_shape=jax.ShapeDtypeStruct((fibers, unknowns), f32),
        in_specs=[vmem, vmem, vmem],
        out_specs=vmem,
        compiler_params=pltpu.CompilerParams(vmem_limit_bytes=8 * 2**20),
    )(at_nodes, tension.reshape(1, nodes), blocks)


def solution(mesh):
    in_specs = (
        P(None, ("aa", "ba")),
        P(None, ("aa", "ba")),
        P(("aa", "ba")),
        P(("aa", "ba")),
        P(("aa", "ba"), None, None),
        P(("aa", "ba"), None, None),
        P(),
        P(("aa", "ba")),
        P(("aa", "ba")),
        P(("aa", "ba"), None),
        P(("aa", "ba"), None, None),
    )
    out_specs = P(("aa", "ba"), None)
    return jax.shard_map(local, mesh=mesh, in_specs=in_specs, out_specs=out_specs, check_vma=False)
```

```python
import functools

import jax
import jax.numpy as jnp
import numpy as np
from jax import lax
from jax.experimental import pallas as pl
from jax.experimental.pallas import tpu as pltpu
from jax.sharding import PartitionSpec as P

MOST = 4
NEAR_SPAN = 128

softening = 0.05
box_margin = 0.05
shell_radius = 2.95
golden_angle = 2.399963229728653
eight_pi = 25.132741228718345
LANES = 128
MESH = pl.DeviceIdType.MESH
f32, bf16, i32 = jnp.float32, jnp.bfloat16, jnp.int32


def surface(amount):
    indices = np.arange(amount, dtype=np.float32) + np.float32(0.5)
    height = np.float32(1.0) - np.float32(2.0) * indices / np.float32(amount)
    radius = np.sqrt(np.maximum(np.float32(1.0) - height * height, np.float32(0.0)))
    azimuth = indices * np.float32(golden_angle)
    spread = np.stack([radius * np.cos(azimuth), radius * np.sin(azimuth), height])
    return jnp.asarray(spread / np.max(np.abs(spread), axis=0, keepdims=True))


def split3_parts(x):
    high = x.astype(bf16).astype(f32)
    rest = x - high
    middle = rest.astype(bf16).astype(f32)
    return [high, middle, rest - middle]


def joined(r):
    n = r.shape[0] // 3
    return r[0:n] + (r[n : 2 * n] + r[2 * n : 3 * n])


def dot_t(a, b):
    return lax.dot_general(a, b, (((1,), (1,)), ((), ())), preferred_element_type=f32)


def dot_n(a, b):
    return lax.dot_general(a, b, (((1,), (0,)), ((), ())), preferred_element_type=f32)


def lane_sums(x):
    ones = jnp.ones((8, x.shape[1]), bf16)
    high = x.astype(bf16)
    rest = x - high.astype(f32)
    return dot_t(ones, high) + dot_t(ones, rest.astype(bf16))


def hot(condition):
    return jnp.where(condition, 1.0, 0.0).astype(bf16)


def body(
    dims,
    fetches,
    slot_ref,
    pos_ref,
    frc_ref,
    lloc_ref,
    par_ref,
    lpar_ref,
    loct_ref,
    near_ref,
    shell_ref,
    maps_hbm,
    out_ref,
    maps_v,
    rank_hot,
    stage,
    flat,
    send,
    recv,
    mine,
    wide,
    rep,
    spots,
    parw,
    trans,
    dens,
    acc,
    rsend,
    rrecv,
    local_sem,
    a_send,
    a_recv,
    p_send,
    p_recv,
    h_send,
    h_recv,
    r_send,
    r_recv,
):
    major, minor, reach = dims
    D = major * minor
    nodes = slot_ref.shape[1]
    cap = MOST * (nodes // D)
    per = LANES // cap
    tiles = D * cap // LANES
    slots = D * cap
    leaves = lloc_ref.shape[1]
    points = nodes // leaves
    node_tiles = nodes // LANES
    in_tile = LANES // points
    near_count = near_ref.shape[1]
    n_par = par_ref.shape[1]
    folds, rows_sent = send_form(cap)
    me = lax.axis_index("aa") * minor + lax.axis_index("ba")

    def dev(t):
        return (lax.div(t, minor), lax.rem(t, minor))

    def partner(k):
        return me ^ (D - k)

    maps_copy = pltpu.make_async_copy(maps_hbm, maps_v, local_sem.at[0])
    barrier = pltpu.get_barrier_semaphore()
    for fetch in fetches[0:3]:
        fetch.start()

    @pl.loop(1, D)
    def _(k):
        pl.semaphore_signal(
            barrier, inc=1, device_id=dev(partner(k)), device_id_type=MESH
        )

    for fetch in fetches[3:]:
        fetch.start()
    maps_copy.start()
    for fetch in fetches[0:3]:
        fetch.wait()

    def owner_of(slot):
        return jnp.floor((slot + 0.5) * (1.0 / nodes))

    def rows_of(shape, group=1):
        row = lax.broadcasted_iota(i32, shape, 0)
        return (row // group if group > 1 else row).astype(f32)

    slot_f = slot_ref[...].astype(f32)
    owner = owner_of(slot_f)
    within = slot_f - owner * nodes
    tile_at = jnp.floor((within + 0.5) * (1.0 / LANES))
    stage[0:3, :] = pos_ref[...]
    stage[3:6, :] = frc_ref[...]
    stage[6:7, :] = within - tile_at * LANES + 1.0
    stage[7:8, :] = tile_at

    owns = jnp.where(rows_of((D, nodes)) == owner, 1.0, 0.0)
    by_tile = [owns[:, t * LANES : (t + 1) * LANES] for t in range(node_tiles)]
    square = (LANES, 2 * LANES)
    over = lax.broadcasted_iota(i32, square, 1)
    before = hot((lax.broadcasted_iota(i32, square, 0) < over) | (over >= LANES))
    counts = dot_n(jnp.concatenate(by_tile, axis=0).astype(bf16), before)
    ranks, base = [], jnp.zeros((D, LANES), f32)
    for t in range(node_tiles):
        at = slice(t * D, (t + 1) * D)
        ranks.append(
            jnp.sum(by_tile[t] * (counts[at, 0:LANES] + base), axis=0, keepdims=True)
        )
        base = base + counts[at, LANES : 2 * LANES]
    rank = jnp.concatenate(ranks, axis=1)
    lane_ids = rows_of((LANES, nodes))
    for g in range(per):
        rank_hot[g] = hot(lane_ids == rank + float(g * cap))

    pieces = split3_parts(stage[...])
    sent = D * rows_sent
    mask = hot(rows_of((sent, nodes), rows_sent) == owner)
    lhs = []
    for piece in pieces:
        folded = []
        for h in range(folds):
            rows = piece[h * rows_sent : (h + 1) * rows_sent]
            rows = jnp.concatenate([rows] * (16 // rows_sent), axis=0).astype(bf16)
            folded.append(
                jnp.concatenate(
                    [mask[b : b + 16] * rows for b in range(0, sent, 16)], axis=0
                )
            )
        lhs.append(jnp.concatenate(folded, axis=1) if folds > 1 else folded[0])
    places = [rank_hot[h] for h in range(folds)]
    packed = joined(
        dot_t(
            jnp.concatenate(lhs, axis=0),
            jnp.concatenate(places, axis=1) if folds > 1 else places[0],
        )
    )
    for o in range(D):
        send[o] = packed[o * rows_sent : (o + 1) * rows_sent]

    pl.semaphore_wait(barrier, D - 1)

    def a2a(src, dst, s_sem, r_sem, group, to, index):
        return pltpu.make_async_remote_copy(
            src_ref=src.at[index],
            dst_ref=dst.at[me],
            send_sem=s_sem.at[group],
            recv_sem=r_sem.at[group],
            device_id=dev(to),
            device_id_type=MESH,
        )

    def all_of(dst, s_sem, r_sem, group, amount):
        whole = dst.at[pl.ds(0, amount)]
        return pltpu.make_async_remote_copy(
            src_ref=whole,
            dst_ref=whole,
            send_sem=s_sem.at[group],
            recv_sem=r_sem.at[group],
            device_id=dev(lax.rem(me + 1, D)),
            device_id_type=MESH,
        )

    @pl.loop(1, D)
    def _(k):
        to = partner(k)
        a2a(send, recv, a_send, a_recv, 0, to, to).start()

    def par_copy(step):
        return pltpu.make_async_remote_copy(
            src_ref=par_ref,
            dst_ref=parw.at[1 - step],
            send_sem=p_send.at[1 - step],
            recv_sem=p_recv.at[1 - step],
            device_id=dev(lax.rem(me + D + step, D)),
            device_id_type=MESH,
        )

    for fetch in fetches[3:]:
        fetch.wait()
    par_copy(1).start()
    par_copy(-1).start()
    recv[me] = send[me]
    parw[1] = par_ref[...]

    half_lanes = lax.broadcasted_iota(i32, (4, LANES), 1) < cap
    all_of(recv, a_send, a_recv, 0, D - 1).wait_recv()

    for t in range(tiles):
        at = slice(t * LANES, (t + 1) * LANES)
        if folds == 2:
            a, b = recv[2 * t], recv[2 * t + 1]
            flat[0:4, at] = jnp.where(half_lanes, a, pltpu.roll(b, cap, 1))
            flat[4:8, at] = jnp.where(half_lanes, pltpu.roll(a, cap, 1), b)
        else:
            total = recv[t * per]
            for g in range(1, per):
                total = total + pltpu.roll(recv[t * per + g], g * cap, 1)
            flat[:, at] = total
    arrived = split3_parts(flat[...])
    lane_hot = hot(rows_of((LANES, slots)) + 1.0 == flat[6:7, :])
    tile_row = flat[7:8, :]
    masked = [
        jnp.where(tile_row == float(t), part, 0.0)
        for t in range(node_tiles)
        for part in arrived
    ]
    placed = dot_t(jnp.concatenate(masked, axis=0).astype(bf16), lane_hot)
    unit = jnp.where(
        lax.broadcasted_iota(i32, (8, LANES), 0) < 3, 1.0 / softening, 1.0
    )
    placed_tiles = [joined(placed[24 * t : 24 * t + 24]) * unit for t in range(node_tiles)]
    last = placed_tiles[-1]
    for t in range(node_tiles - 1):
        mine[8 * t : 8 * t + 6, :] = placed_tiles[t][0:6]
        mine[8 * t + 6 : 8 * t + 8, :] = last[2 * t : 2 * t + 2]

    def halo(k, act):
        there = me - k if act == "wait_recv" else me + k

        @pl.when((there >= 0) & (there < D))
        def _():
            copy = pltpu.make_async_remote_copy(
                src_ref=mine,
                dst_ref=wide.at[reach - k],
                send_sem=h_send.at[reach - k],
                recv_sem=h_recv.at[reach - k],
                device_id=dev(there),
                device_id_type=MESH,
            )
            getattr(copy, act)()

    @pl.loop(0, reach)
    def _(j):
        halo(reach - j, "start")
        halo(j - reach, "start")

    wide[reach] = mine[...]
    for t in range(node_tiles):
        turned = jnp.transpose(placed_tiles[t])
        at = slice(t * LANES, (t + 1) * LANES)
        for c in range(3):
            spots[c, at, :] = jnp.broadcast_to(turned[:, c : c + 1], (LANES, LANES))

    par_copy(1).wait()
    par_copy(-1).wait()
    diagonal_of = (leaves, leaves)
    diagonal = lax.broadcasted_iota(i32, diagonal_of, 0) == lax.broadcasted_iota(
        i32, diagonal_of, 1
    )

    def column(row):
        return jnp.sum(jnp.where(diagonal, row.astype(f32), 0.0), axis=1, keepdims=True)

    wanted = column(lpar_ref[...] - (me - 1) * n_par)
    parts = []
    for c in range(3):
        total = jnp.zeros((leaves, LANES), f32)
        for j in range(3 * n_par):
            row = parw[j // n_par, c, j % n_par : j % n_par + 1, :]
            total = jnp.where(wanted == j, row, total)
        parts.append(total)
    wide_row = jnp.concatenate(parts, axis=1)
    high = wide_row.astype(bf16)
    low = (wide_row - high.astype(f32)).astype(bf16)
    both = jnp.concatenate([high, low], axis=0)
    octant = column(loct_ref[...])

    maps_copy.wait()
    trans[...] = jnp.zeros(trans.shape, f32)

    @pl.loop(0, maps_v.shape[0])
    def _(o):
        m = maps_v[o]
        m_high = m.astype(bf16)
        m_low = (m - m_high.astype(f32)).astype(bf16)
        first = dot_t(both, m_high)
        image = first[0:leaves] + (first[leaves : 2 * leaves] + dot_t(high, m_low))
        trans[...] = jnp.where(octant == jnp.asarray(o, i32).astype(f32), image, trans[...])

    for c in range(3):
        dens[c] = lloc_ref[c] + trans[:, c * LANES : (c + 1) * LANES]

    def pair_sums(targets, gaps_from, strengths, soft_by, sums):
        gap = [targets[c] - gaps_from[c] for c in range(3)]
        d2 = gap[0] * gap[0] + gap[1] * gap[1] + gap[2] * gap[2]
        soft = d2 + 1.0 if soft_by else d2
        inverse = lax.rsqrt(soft)
        weight = inverse * inverse * inverse
        along = gap[0] * strengths[0] + gap[1] * strengths[1] + gap[2] * strengths[2]
        near = inverse + weight if soft_by else inverse
        along = along * weight
        return [sums[c] + (near * strengths[c] + along * gap[c]) for c in range(3)]

    def leaf_rows(leaf):
        return pl.ds(pl.multiple_of(leaf * points, points), points)

    @pl.loop(0, leaves)
    def _(leaf):
        at = leaf_rows(leaf)
        targets = [spots[c, at, :] for c in range(3)]
        center = [jnp.sum(x, axis=0, keepdims=True) * (1.0 / points) for x in targets]
        spread = [
            jnp.max(jnp.abs(targets[c] - center[c]), axis=0, keepdims=True) for c in range(3)
        ]
        half = jnp.maximum(jnp.maximum(spread[0], spread[1]), spread[2])
        half = half + box_margin / softening
        points_at = [
            center[c] + shell_radius * half * shell_ref[c : c + 1, :] for c in range(3)
        ]
        density = [dens[c, pl.ds(leaf, 1), :] for c in range(3)]
        zero = jnp.zeros((points, LANES), f32)
        sums = pair_sums(targets, points_at, density, False, [zero, zero, zero])
        for c in range(3):
            acc[c, at, :] = sums[c]

    lane_group = lax.broadcasted_iota(i32, (8, LANES), 1) // points

    def spread_out(j):
        for t in range(node_tiles):
            if t < node_tiles - 1:
                tile = wide[j, 8 * t : 8 * t + 8, :]
            else:
                ends = [wide[j, 8 * i + 6 : 8 * i + 8, :] for i in range(node_tiles - 1)]
                tile = jnp.concatenate(ends + ends[0:1], axis=0)
            turned = [tile] + [pltpu.roll(tile, s * points, 1) for s in range(1, in_tile)]
            for i in range(in_tile):
                full = turned[(-i) % in_tile]
                for g in range(1, in_tile):
                    full = jnp.where(lane_group == g, turned[(g - i) % in_tile], full)
                rep[j * leaves + t * in_tile + i] = full

    spread_out(reach)
    together = 2 if reach % 2 == 0 else 1

    @pl.loop(0, reach // together)
    def _(step):
        ks = [step * together + 1 + i for i in range(together)]
        for k in ks:
            halo(k, "wait_recv")
            halo(-k, "wait_recv")
        for k in ks:
            spread_out(reach - k)
            spread_out(reach + k)

    first_leaf = (me - reach) * leaves

    def table_row(leaf, n):
        row = near_ref[leaf, n] - first_leaf
        return jnp.minimum(jnp.maximum(row, 0), rep.shape[0] - 1)

    def near_field(leaf):
        at = leaf_rows(leaf)
        targets = [spots[c, at, :] for c in range(3)]
        sums = [acc[c, at, :] for c in range(3)]
        for base in range(0, near_count, in_tile):
            count = min(in_tile, near_count - base)
            source = rep[table_row(leaf, base)]
            for g in range(1, count):
                source = jnp.where(lane_group == g, rep[table_row(leaf, base + g)], source)
            if count < in_tile:
                row = lax.broadcasted_iota(i32, (8, LANES), 0)
                source = jnp.where((lane_group >= count) & (row >= 3), 0.0, source)
            sums = pair_sums(
                targets,
                [source[c : c + 1] for c in range(3)],
                [source[c + 3 : c + 4] for c in range(3)],
                True,
                sums,
            )
        for c in range(3):
            acc[c, at, :] = sums[c]

    @pl.loop(0, node_tiles)
    def _(t):
        for i in range(in_tile):
            near_field(t * in_tile + i)
        at = pl.ds(pl.multiple_of(t * LANES, LANES), LANES)
        for row, c in ((0, 0), (1, 2), (2, 1)):
            speed = jnp.sum(jnp.transpose(acc[c, at, :]), axis=0, keepdims=True)
            stage[row : row + 1, at] = speed * (1.0 / (eight_pi * softening))

    stage[3:4, :] = jnp.zeros((1, nodes), f32)
    pairs = [
        jnp.concatenate(
            [stage[0:4, t * LANES : (t + 1) * LANES] for t in range(p, p + 2)], axis=0
        )
        for p in range(0, node_tiles, 2)
    ]
    for t in range(tiles):
        at = slice(t * LANES, (t + 1) * LANES)
        lane = jnp.maximum(flat[6:7, at] - 1.0, 0.0).astype(i32)
        lane = jnp.broadcast_to(lane, (8, LANES))
        tile = flat[7:8, at]
        found = jnp.take_along_axis(pairs[0], lane, axis=1)
        for p in range(1, len(pairs)):
            more = jnp.take_along_axis(pairs[p], lane, axis=1)
            found = jnp.where(tile >= float(2 * p), more, found)
        even = jnp.floor(tile * 0.5) * 2.0
        found = jnp.where(tile > even, found[4:8], found[0:4])
        if folds == 2:
            turned = pltpu.roll(found, cap, 1)
            left = half_lanes[0:2]
            rsend[2 * t] = jnp.where(left, found[0:2], turned[2:4])
            rsend[2 * t + 1] = jnp.where(left, turned[0:2], found[2:4])
        else:
            for g in range(per):
                rsend[t * per + g] = pltpu.roll(found, (LANES - g * cap) % LANES, 1)

    @pl.loop(1, D)
    def _(k):
        to = partner(k)
        a2a(rsend, rrecv, r_send, r_recv, 0, to, to).start()

    rrecv[me] = rsend[me]

    all_of(recv, a_send, a_recv, 0, D - 1).wait_send()

    @pl.loop(1, reach + 1)
    def _(k):
        halo(k, "wait_send")
        halo(-k, "wait_send")

    all_of(rrecv, r_send, r_recv, 0, D - 1).wait_recv()

    got = jnp.concatenate([rrecv[o] for o in range(D)], axis=0)
    got_high = got.astype(bf16)
    got_low = (got - got_high.astype(f32)).astype(bf16)
    sides = [rank_hot[h] for h in range(folds)]
    found = dot_n(
        jnp.concatenate([got_high, got_low], axis=0),
        jnp.concatenate(sides, axis=1) if folds > 1 else sides[0],
    )
    back = 4 // folds
    owner = owner_of(slot_ref[...].astype(f32))
    owner = jnp.concatenate([owner] * folds, axis=1)
    owner_rows = rows_of((8, folds * nodes), back)
    total = jnp.zeros((8, folds * nodes), f32)
    for b in range(0, D * back, 8):
        both_rows = found[b : b + 8] + found[D * back + b : D * back + b + 8]
        total = jnp.where(owner_rows + float(b // back) == owner, both_rows, total)
    while total.shape[0] > back:
        middle = total.shape[0] // 2
        total = total[0:middle] + total[middle:]
    out_ref[0:back, :] = total[:, 0:nodes]
    if folds > 1:
        out_ref[back : 2 * back, :] = total[:, nodes:]

    all_of(rrecv, r_send, r_recv, 0, D - 1).wait_send()


def final(nodes_ref, ten_ref, blocks_v, out_ref):
    at_nodes = nodes_ref[...]
    fibers = blocks_v.shape[0]
    npf = at_nodes.shape[1] // fibers
    per_tile = LANES // npf
    left = lax.broadcasted_iota(i32, (1, LANES), 1) < npf
    for i in range(fibers):
        t, g = i // per_tile, i % per_tile
        lanes = slice(t * LANES, (t + 1) * LANES)
        x, z, y = (at_nodes[c : c + 1, lanes] for c in range(3))
        tension = ten_ref[0:1, lanes]

        def side(v, to):
            turn = ((to - g) * npf) % LANES
            return pltpu.roll(v, turn, 1) if turn else v

        first = jnp.where(left, side(x, 0), side(y, 1))
        second = jnp.where(left, side(z, 0), side(tension, 1))
        products = blocks_v[i, :, 0:LANES] * first + blocks_v[i, :, LANES : 2 * LANES] * second
        out_ref[i : i + 1, :] = lane_sums(products)[0:1]


def send_form(cap):
    folds = 2 if LANES == 2 * cap else 1
    return folds, 8 // folds


def kernel(dims, count, *refs):
    given, held = refs[0:count], refs[count + 2 : 2 * count + 2]
    fetch_sem = refs[-1]
    fetches = [
        pltpu.make_async_copy(given[n], held[n], fetch_sem.at[n]) for n in range(count)
    ]
    body(dims, fetches, *held, *refs[count : count + 2], *refs[2 * count + 2 : -1])


def local(
    positions,
    forces,
    tension,
    node_slot,
    leaf_local,
    parent_local,
    l2l_maps,
    leaf_parent,
    leaf_octant,
    near_list,
    blocks,
):
    major, minor = lax.axis_size("aa"), lax.axis_size("ba")
    D = major * minor
    nodes = node_slot.shape[0]
    leaves, _, shell = leaf_local.shape
    reach = -(-NEAR_SPAN // leaves)
    cap = MOST * (nodes // D)
    slots = D * cap
    fibers, unknowns, _ = blocks.shape
    node_tiles = nodes // LANES
    _, rows_sent = send_form(cap)
    vmem = pl.BlockSpec(memory_space=pltpu.VMEM)
    anywhere = pl.BlockSpec(memory_space=pl.ANY)
    dma = pltpu.SemaphoreType.DMA
    operands = (
        node_slot.reshape(1, nodes),
        positions,
        forces,
        leaf_local.transpose(1, 0, 2),
        parent_local.transpose(1, 0, 2),
        leaf_parent.reshape(1, leaves),
        leaf_octant.reshape(1, leaves),
        near_list,
        surface(shell),
    )
    held = [
        (pltpu.SMEM if x is near_list else pltpu.VMEM)(x.shape, x.dtype) for x in operands
    ]
    at_nodes = pl.pallas_call(
        functools.partial(kernel, (major, minor, reach), len(operands)),
        out_shape=pltpu.VMEM((4, nodes), f32),
        in_specs=[anywhere] * (len(operands) + 1),
        out_specs=vmem,
        scratch_shapes=held
        + [
            pltpu.VMEM(l2l_maps.shape, f32),
            pltpu.VMEM((LANES // cap, LANES, nodes), bf16),
            pltpu.VMEM((8, nodes), f32),
            pltpu.VMEM((8, slots), f32),
            pltpu.VMEM((D, rows_sent, LANES), f32),
            pltpu.VMEM((D, rows_sent, LANES), f32),
            pltpu.VMEM((8 * (node_tiles - 1), LANES), f32),
            pltpu.VMEM((2 * reach + 1, 8 * (node_tiles - 1), LANES), f32),
            pltpu.VMEM(((2 * reach + 1) * leaves, 8, LANES), f32),
            pltpu.VMEM((3, nodes, LANES), f32),
            pltpu.VMEM((3, 3, parent_local.shape[0], shell), f32),
            pltpu.VMEM((leaves, 3 * shell), f32),
            pltpu.VMEM((3, leaves, shell), f32),
            pltpu.VMEM((3, nodes, LANES), f32),
            pltpu.VMEM((D, rows_sent // 2, LANES), f32),
            pltpu.VMEM((D, rows_sent // 2, LANES), f32),
            dma((1,)),
            dma((2,)),
            dma((2,)),
            dma((3,)),
            dma((3,)),
            dma((2 * reach + 1,)),
            dma((2 * reach + 1,)),
            dma((1,)),
            dma((1,)),
            dma((len(operands),)),
        ],
        compiler_params=pltpu.CompilerParams(
            collective_id=0, has_side_effects=True, vmem_limit_bytes=56 * 2**20
        ),
    )(*operands, l2l_maps)
    return pl.pallas_call(
        final,
        out_shape=jax.ShapeDtypeStruct((fibers, unknowns), f32),
        in_specs=[vmem, vmem, vmem],
        out_specs=vmem,
        compiler_params=pltpu.CompilerParams(vmem_limit_bytes=8 * 2**20),
    )(at_nodes, tension.reshape(1, nodes), blocks)


def solution(mesh):
    in_specs = (
        P(None, ("aa", "ba")),
        P(None, ("aa", "ba")),
        P(("aa", "ba")),
        P(("aa", "ba")),
        P(("aa", "ba"), None, None),
        P(("aa", "ba"), None, None),
        P(),
        P(("aa", "ba")),
        P(("aa", "ba")),
        P(("aa", "ba"), None),
        P(("aa", "ba"), None, None),
    )
    out_specs = P(("aa", "ba"), None)
    return jax.shard_map(local, mesh=mesh, in_specs=in_specs, out_specs=out_specs, check_vma=False)
```

```python
import functools

import jax
import jax.numpy as jnp
import numpy as np
from jax import lax
from jax.experimental import pallas as pl
from jax.experimental.pallas import tpu as pltpu
from jax.sharding import PartitionSpec as P

MOST = 4
NEAR_SPAN = 128

softening = 0.05
box_margin = 0.05
shell_radius = 2.95
golden_angle = 2.399963229728653
eight_pi = 25.132741228718345
LANES = 128
MESH = pl.DeviceIdType.MESH
f32, bf16, i32 = jnp.float32, jnp.bfloat16, jnp.int32


def surface(amount):
    indices = np.arange(amount, dtype=np.float32) + np.float32(0.5)
    height = np.float32(1.0) - np.float32(2.0) * indices / np.float32(amount)
    radius = np.sqrt(np.maximum(np.float32(1.0) - height * height, np.float32(0.0)))
    azimuth = indices * np.float32(golden_angle)
    spread = np.stack([radius * np.cos(azimuth), radius * np.sin(azimuth), height])
    return jnp.asarray(spread / np.max(np.abs(spread), axis=0, keepdims=True))


def split3_parts(x):
    high = x.astype(bf16).astype(f32)
    rest = x - high
    middle = rest.astype(bf16).astype(f32)
    return [high, middle, rest - middle]


def joined(r):
    n = r.shape[0] // 3
    return r[0:n] + (r[n : 2 * n] + r[2 * n : 3 * n])


def dot_t(a, b):
    return lax.dot_general(a, b, (((1,), (1,)), ((), ())), preferred_element_type=f32)


def dot_n(a, b):
    return lax.dot_general(a, b, (((1,), (0,)), ((), ())), preferred_element_type=f32)


def hot(condition):
    return jnp.where(condition, 1.0, 0.0).astype(bf16)


def body(
    dims,
    fetches,
    slot_ref,
    pos_ref,
    frc_ref,
    lloc_ref,
    par_ref,
    lpar_ref,
    loct_ref,
    near_ref,
    shell_ref,
    maps_hbm,
    out_ref,
    maps_v,
    rank_hot,
    stage,
    flat,
    send,
    recv,
    mine,
    wide,
    rep,
    spots,
    parw,
    trans,
    dens,
    acc,
    rsend,
    rrecv,
    local_sem,
    a_send,
    a_recv,
    p_send,
    p_recv,
    h_send,
    h_recv,
    r_send,
    r_recv,
):
    major, minor, reach = dims
    D = major * minor
    nodes = slot_ref.shape[1]
    cap = MOST * (nodes // D)
    per = LANES // cap
    tiles = D * cap // LANES
    slots = D * cap
    leaves = lloc_ref.shape[1]
    points = nodes // leaves
    node_tiles = nodes // LANES
    in_tile = LANES // points
    near_count = near_ref.shape[1]
    n_par = par_ref.shape[1]
    folds, rows_sent = send_form(cap)
    me = lax.axis_index("aa") * minor + lax.axis_index("ba")

    def dev(t):
        return (lax.div(t, minor), lax.rem(t, minor))

    def partner(k):
        return me ^ (D - k)

    maps_copy = pltpu.make_async_copy(maps_hbm, maps_v, local_sem.at[0])
    barrier = pltpu.get_barrier_semaphore()
    for fetch in fetches[0:3]:
        fetch.start()

    @pl.loop(1, D)
    def _(k):
        pl.semaphore_signal(
            barrier, inc=1, device_id=dev(partner(k)), device_id_type=MESH
        )

    for fetch in fetches[3:]:
        fetch.start()
    maps_copy.start()
    for fetch in fetches[0:3]:
        fetch.wait()

    def owner_of(slot):
        return jnp.floor((slot + 0.5) * (1.0 / nodes))

    def rows_of(shape, group=1):
        row = lax.broadcasted_iota(i32, shape, 0)
        return (row // group if group > 1 else row).astype(f32)

    slot_f = slot_ref[...].astype(f32)
    owner = owner_of(slot_f)
    within = slot_f - owner * nodes
    tile_at = jnp.floor((within + 0.5) * (1.0 / LANES))
    stage[0:3, :] = pos_ref[...]
    stage[3:6, :] = frc_ref[...]
    stage[6:7, :] = within - tile_at * LANES + 1.0
    stage[7:8, :] = tile_at

    owns = jnp.where(rows_of((D, nodes)) == owner, 1.0, 0.0)
    by_tile = [owns[:, t * LANES : (t + 1) * LANES] for t in range(node_tiles)]
    square = (LANES, 2 * LANES)
    over = lax.broadcasted_iota(i32, square, 1)
    before = hot((lax.broadcasted_iota(i32, square, 0) < over) | (over >= LANES))
    counts = dot_n(jnp.concatenate(by_tile, axis=0).astype(bf16), before)
    ranks, base = [], jnp.zeros((D, LANES), f32)
    for t in range(node_tiles):
        at = slice(t * D, (t + 1) * D)
        ranks.append(
            jnp.sum(by_tile[t] * (counts[at, 0:LANES] + base), axis=0, keepdims=True)
        )
        base = base + counts[at, LANES : 2 * LANES]
    rank = jnp.concatenate(ranks, axis=1)
    lane_ids = rows_of((LANES, nodes))
    for g in range(per):
        rank_hot[g] = hot(lane_ids == rank + float(g * cap))

    pieces = split3_parts(stage[...])
    sent = D * rows_sent
    mask = hot(rows_of((sent, nodes), rows_sent) == owner)
    lhs = []
    for piece in pieces:
        folded = []
        for h in range(folds):
            rows = piece[h * rows_sent : (h + 1) * rows_sent]
            rows = jnp.concatenate([rows] * (16 // rows_sent), axis=0).astype(bf16)
            folded.append(
                jnp.concatenate(
                    [mask[b : b + 16] * rows for b in range(0, sent, 16)], axis=0
                )
            )
        lhs.append(jnp.concatenate(folded, axis=1) if folds > 1 else folded[0])
    places = [rank_hot[h] for h in range(folds)]
    packed = joined(
        dot_t(
            jnp.concatenate(lhs, axis=0),
            jnp.concatenate(places, axis=1) if folds > 1 else places[0],
        )
    )
    for o in range(D):
        send[o] = packed[o * rows_sent : (o + 1) * rows_sent]

    pl.semaphore_wait(barrier, D - 1)

    def a2a(src, dst, s_sem, r_sem, group, to, index):
        return pltpu.make_async_remote_copy(
            src_ref=src.at[index],
            dst_ref=dst.at[me],
            send_sem=s_sem.at[group],
            recv_sem=r_sem.at[group],
            device_id=dev(to),
            device_id_type=MESH,
        )

    def all_of(dst, s_sem, r_sem, group, amount):
        whole = dst.at[pl.ds(0, amount)]
        return pltpu.make_async_remote_copy(
            src_ref=whole,
            dst_ref=whole,
            send_sem=s_sem.at[group],
            recv_sem=r_sem.at[group],
            device_id=dev(lax.rem(me + 1, D)),
            device_id_type=MESH,
        )

    @pl.loop(1, D)
    def _(k):
        to = partner(k)
        a2a(send, recv, a_send, a_recv, 0, to, to).start()

    def par_copy(step):
        return pltpu.make_async_remote_copy(
            src_ref=par_ref,
            dst_ref=parw.at[1 - step],
            send_sem=p_send.at[1 - step],
            recv_sem=p_recv.at[1 - step],
            device_id=dev(lax.rem(me + D + step, D)),
            device_id_type=MESH,
        )

    for fetch in fetches[3:]:
        fetch.wait()
    par_copy(1).start()
    par_copy(-1).start()
    recv[me] = send[me]
    parw[1] = par_ref[...]

    half_lanes = lax.broadcasted_iota(i32, (4, LANES), 1) < cap
    all_of(recv, a_send, a_recv, 0, D - 1).wait_recv()

    for t in range(tiles):
        at = slice(t * LANES, (t + 1) * LANES)
        if folds == 2:
            a, b = recv[2 * t], recv[2 * t + 1]
            flat[0:4, at] = jnp.where(half_lanes, a, pltpu.roll(b, cap, 1))
            flat[4:8, at] = jnp.where(half_lanes, pltpu.roll(a, cap, 1), b)
        else:
            total = recv[t * per]
            for g in range(1, per):
                total = total + pltpu.roll(recv[t * per + g], g * cap, 1)
            flat[:, at] = total
    arrived = split3_parts(flat[...])
    lane_hot = hot(rows_of((LANES, slots)) + 1.0 == flat[6:7, :])
    tile_row = flat[7:8, :]
    masked = [
        jnp.where(tile_row == float(t), part, 0.0)
        for t in range(node_tiles)
        for part in arrived
    ]
    placed = dot_t(jnp.concatenate(masked, axis=0).astype(bf16), lane_hot)
    unit = jnp.where(
        lax.broadcasted_iota(i32, (8, LANES), 0) < 3, 1.0 / softening, 1.0
    )
    placed_tiles = [joined(placed[24 * t : 24 * t + 24]) * unit for t in range(node_tiles)]
    last = placed_tiles[-1]
    for t in range(node_tiles - 1):
        mine[8 * t : 8 * t + 6, :] = placed_tiles[t][0:6]
        mine[8 * t + 6 : 8 * t + 8, :] = last[2 * t : 2 * t + 2]

    def halo(k, act):
        there = me - k if act == "wait_recv" else me + k

        @pl.when((there >= 0) & (there < D))
        def _():
            copy = pltpu.make_async_remote_copy(
                src_ref=mine,
                dst_ref=wide.at[reach - k],
                send_sem=h_send.at[reach - k],
                recv_sem=h_recv.at[reach - k],
                device_id=dev(there),
                device_id_type=MESH,
            )
            getattr(copy, act)()

    for k in sorted(range(1, reach + 1), key=lambda k: (abs(2 * k - reach), -k)):
        halo(k, "start")
        halo(-k, "start")

    wide[reach] = mine[...]
    for t in range(node_tiles):
        turned = jnp.transpose(placed_tiles[t])
        at = slice(t * LANES, (t + 1) * LANES)
        for c in range(3):
            spots[c, at, :] = jnp.broadcast_to(turned[:, c : c + 1], (LANES, LANES))

    par_copy(1).wait()
    par_copy(-1).wait()
    diagonal_of = (leaves, leaves)
    diagonal = lax.broadcasted_iota(i32, diagonal_of, 0) == lax.broadcasted_iota(
        i32, diagonal_of, 1
    )

    def column(row):
        return jnp.sum(jnp.where(diagonal, row.astype(f32), 0.0), axis=1, keepdims=True)

    wanted = column(lpar_ref[...] - (me - 1) * n_par)
    parts = []
    for c in range(3):
        total = jnp.zeros((leaves, LANES), f32)
        for j in range(3 * n_par):
            row = parw[j // n_par, c, j % n_par : j % n_par + 1, :]
            total = jnp.where(wanted == j, row, total)
        parts.append(total)
    wide_row = jnp.concatenate(parts, axis=1)
    high = wide_row.astype(bf16)
    low = (wide_row - high.astype(f32)).astype(bf16)
    both = jnp.concatenate([high, low], axis=0)
    octant = column(loct_ref[...])

    maps_copy.wait()
    trans[...] = jnp.zeros(trans.shape, f32)

    @pl.loop(0, maps_v.shape[0])
    def _(o):
        m = maps_v[o]
        m_high = m.astype(bf16)
        m_low = (m - m_high.astype(f32)).astype(bf16)
        first = dot_t(both, m_high)
        image = first[0:leaves] + (first[leaves : 2 * leaves] + dot_t(high, m_low))
        trans[...] = jnp.where(octant == jnp.asarray(o, i32).astype(f32), image, trans[...])

    for c in range(3):
        dens[c] = lloc_ref[c] + trans[:, c * LANES : (c + 1) * LANES]

    def pair_sums(targets, gaps_from, strengths, soft_by, sums):
        gap = [targets[c] - gaps_from[c] for c in range(3)]
        d2 = gap[0] * gap[0] + gap[1] * gap[1] + gap[2] * gap[2]
        soft = d2 + 1.0 if soft_by else d2
        inverse = lax.rsqrt(soft)
        weight = inverse * inverse * inverse
        along = gap[0] * strengths[0] + gap[1] * strengths[1] + gap[2] * strengths[2]
        near = inverse + weight if soft_by else inverse
        along = along * weight
        return [sums[c] + (near * strengths[c] + along * gap[c]) for c in range(3)]

    def leaf_rows(leaf):
        return pl.ds(pl.multiple_of(leaf * points, points), points)

    @pl.loop(0, leaves)
    def _(leaf):
        at = leaf_rows(leaf)
        targets = [spots[c, at, :] for c in range(3)]
        center = [jnp.sum(x, axis=0, keepdims=True) * (1.0 / points) for x in targets]
        spread = [
            jnp.max(jnp.abs(targets[c] - center[c]), axis=0, keepdims=True) for c in range(3)
        ]
        half = jnp.maximum(jnp.maximum(spread[0], spread[1]), spread[2])
        half = half + box_margin / softening
        points_at = [
            center[c] + shell_radius * half * shell_ref[c : c + 1, :] for c in range(3)
        ]
        density = [dens[c, pl.ds(leaf, 1), :] for c in range(3)]
        zero = jnp.zeros((points, LANES), f32)
        sums = pair_sums(targets, points_at, density, False, [zero, zero, zero])
        for c in range(3):
            acc[c, at, :] = sums[c]

    lane_group = lax.broadcasted_iota(i32, (8, LANES), 1) // points

    def spread_out(j):
        for t in range(node_tiles):
            if t < node_tiles - 1:
                tile = wide[j, 8 * t : 8 * t + 8, :]
            else:
                ends = [wide[j, 8 * i + 6 : 8 * i + 8, :] for i in range(node_tiles - 1)]
                tile = jnp.concatenate(ends + ends[0:1], axis=0)
            turned = [tile] + [pltpu.roll(tile, s * points, 1) for s in range(1, in_tile)]
            for i in range(in_tile):
                full = turned[(-i) % in_tile]
                for g in range(1, in_tile):
                    full = jnp.where(lane_group == g, turned[(g - i) % in_tile], full)
                rep[j * leaves + t * in_tile + i] = full

    spread_out(reach)
    together = 2 if reach % 2 == 0 else 1

    @pl.loop(0, reach // together)
    def _(step):
        ks = [step * together + 1 + i for i in range(together)]
        for k in ks:
            halo(k, "wait_recv")
            halo(-k, "wait_recv")
        for k in ks:
            spread_out(reach - k)
            spread_out(reach + k)

    first_leaf = (me - reach) * leaves

    def table_row(leaf, n):
        row = near_ref[leaf, n] - first_leaf
        return jnp.minimum(jnp.maximum(row, 0), rep.shape[0] - 1)

    def near_field(leaf):
        at = leaf_rows(leaf)
        targets = [spots[c, at, :] for c in range(3)]
        sums = [acc[c, at, :] for c in range(3)]
        for base in range(0, near_count, in_tile):
            count = min(in_tile, near_count - base)
            source = rep[table_row(leaf, base)]
            for g in range(1, count):
                source = jnp.where(lane_group == g, rep[table_row(leaf, base + g)], source)
            if count < in_tile:
                row = lax.broadcasted_iota(i32, (8, LANES), 0)
                source = jnp.where((lane_group >= count) & (row >= 3), 0.0, source)
            sums = pair_sums(
                targets,
                [source[c : c + 1] for c in range(3)],
                [source[c + 3 : c + 4] for c in range(3)],
                True,
                sums,
            )
        for c in range(3):
            acc[c, at, :] = sums[c]

    def row_sums(t):
        at = pl.ds(pl.multiple_of(t * LANES, LANES), LANES)
        for row, c in ((0, 0), (1, 2), (2, 1)):
            speed = jnp.sum(jnp.transpose(acc[c, at, :]), axis=0, keepdims=True)
            stage[row : row + 1, at] = speed * (1.0 / (eight_pi * softening))

    @pl.loop(0, node_tiles)
    def _(t):
        row_sums(jnp.maximum(t - 1, 0))
        for i in range(in_tile):
            near_field(t * in_tile + i)

    row_sums(node_tiles - 1)
    stage[3:4, :] = jnp.zeros((1, nodes), f32)
    pairs = [
        jnp.concatenate(
            [stage[0:4, t * LANES : (t + 1) * LANES] for t in range(p, p + 2)], axis=0
        )
        for p in range(0, node_tiles, 2)
    ]
    for t in range(tiles):
        at = slice(t * LANES, (t + 1) * LANES)
        lane = jnp.maximum(flat[6:7, at] - 1.0, 0.0).astype(i32)
        lane = jnp.broadcast_to(lane, (8, LANES))
        tile = flat[7:8, at]
        found = jnp.take_along_axis(pairs[0], lane, axis=1)
        for p in range(1, len(pairs)):
            more = jnp.take_along_axis(pairs[p], lane, axis=1)
            found = jnp.where(tile >= float(2 * p), more, found)
        even = jnp.floor(tile * 0.5) * 2.0
        found = jnp.where(tile > even, found[4:8], found[0:4])
        if folds == 2:
            turned = pltpu.roll(found, cap, 1)
            left = half_lanes[0:2]
            rsend[2 * t] = jnp.where(left, found[0:2], turned[2:4])
            rsend[2 * t + 1] = jnp.where(left, turned[0:2], found[2:4])
        else:
            for g in range(per):
                rsend[t * per + g] = pltpu.roll(found, (LANES - g * cap) % LANES, 1)

    @pl.loop(1, D)
    def _(k):
        to = partner(k)
        a2a(rsend, rrecv, r_send, r_recv, 0, to, to).start()

    rrecv[me] = rsend[me]

    all_of(recv, a_send, a_recv, 0, D - 1).wait_send()

    @pl.loop(1, reach + 1)
    def _(k):
        halo(k, "wait_send")
        halo(-k, "wait_send")

    all_of(rrecv, r_send, r_recv, 0, D - 1).wait_recv()

    got = jnp.concatenate([rrecv[o] for o in range(D)], axis=0)
    got_high = got.astype(bf16)
    got_low = (got - got_high.astype(f32)).astype(bf16)
    sides = [rank_hot[h] for h in range(folds)]
    found = dot_n(
        jnp.concatenate([got_high, got_low], axis=0),
        jnp.concatenate(sides, axis=1) if folds > 1 else sides[0],
    )
    back = 4 // folds
    owner = owner_of(slot_ref[...].astype(f32))
    owner = jnp.concatenate([owner] * folds, axis=1)
    owner_rows = rows_of((8, folds * nodes), back)
    total = jnp.zeros((8, folds * nodes), f32)
    for b in range(0, D * back, 8):
        both_rows = found[b : b + 8] + found[D * back + b : D * back + b + 8]
        total = jnp.where(owner_rows + float(b // back) == owner, both_rows, total)
    while total.shape[0] > back:
        middle = total.shape[0] // 2
        total = total[0:middle] + total[middle:]
    out_ref[0:back, :] = total[:, 0:nodes]
    if folds > 1:
        out_ref[back : 2 * back, :] = total[:, nodes:]

    all_of(rrecv, r_send, r_recv, 0, D - 1).wait_send()


def final(nodes_ref, ten_ref, blocks_v, out_ref):
    at_nodes = nodes_ref[...]
    fibers = blocks_v.shape[0]
    npf = at_nodes.shape[1] // fibers
    per_tile = LANES // npf
    left = lax.broadcasted_iota(i32, (1, LANES), 1) < npf
    for i in range(fibers):
        t, g = i // per_tile, i % per_tile
        lanes = slice(t * LANES, (t + 1) * LANES)
        x, z, y = (at_nodes[c : c + 1, lanes] for c in range(3))
        tension = ten_ref[0:1, lanes]

        def side(v, to):
            turn = ((to - g) * npf) % LANES
            return pltpu.roll(v, turn, 1) if turn else v

        first = jnp.where(left, side(x, 0), side(y, 1))
        second = jnp.where(left, side(z, 0), side(tension, 1))
        products = blocks_v[i, :, 0:LANES] * first + blocks_v[i, :, LANES : 2 * LANES] * second
        for h in range(0, products.shape[0], LANES):
            turned = jnp.transpose(products[h : h + LANES])
            out_ref[i : i + 1, h : h + LANES] = jnp.sum(turned, axis=0, keepdims=True)


def send_form(cap):
    folds = 2 if LANES == 2 * cap else 1
    return folds, 8 // folds


def kernel(dims, count, *refs):
    given, held = refs[0:count], refs[count + 2 : 2 * count + 2]
    fetch_sem = refs[-1]
    fetches = [
        pltpu.make_async_copy(given[n], held[n], fetch_sem.at[n]) for n in range(count)
    ]
    body(dims, fetches, *held, *refs[count : count + 2], *refs[2 * count + 2 : -1])


def local(
    positions,
    forces,
    tension,
    node_slot,
    leaf_local,
    parent_local,
    l2l_maps,
    leaf_parent,
    leaf_octant,
    near_list,
    blocks,
):
    major, minor = lax.axis_size("aa"), lax.axis_size("ba")
    D = major * minor
    nodes = node_slot.shape[0]
    leaves, _, shell = leaf_local.shape
    reach = -(-NEAR_SPAN // leaves)
    cap = MOST * (nodes // D)
    slots = D * cap
    fibers, unknowns, _ = blocks.shape
    node_tiles = nodes // LANES
    _, rows_sent = send_form(cap)
    vmem = pl.BlockSpec(memory_space=pltpu.VMEM)
    anywhere = pl.BlockSpec(memory_space=pl.ANY)
    dma = pltpu.SemaphoreType.DMA
    operands = (
        node_slot.reshape(1, nodes),
        positions,
        forces,
        leaf_local.transpose(1, 0, 2),
        parent_local.transpose(1, 0, 2),
        leaf_parent.reshape(1, leaves),
        leaf_octant.reshape(1, leaves),
        near_list,
        surface(shell),
    )
    held = [
        (pltpu.SMEM if x is near_list else pltpu.VMEM)(x.shape, x.dtype) for x in operands
    ]
    at_nodes = pl.pallas_call(
        functools.partial(kernel, (major, minor, reach), len(operands)),
        out_shape=pltpu.VMEM((4, nodes), f32),
        in_specs=[anywhere] * (len(operands) + 1),
        out_specs=vmem,
        scratch_shapes=held
        + [
            pltpu.VMEM(l2l_maps.shape, f32),
            pltpu.VMEM((LANES // cap, LANES, nodes), bf16),
            pltpu.VMEM((8, nodes), f32),
            pltpu.VMEM((8, slots), f32),
            pltpu.VMEM((D, rows_sent, LANES), f32),
            pltpu.VMEM((D, rows_sent, LANES), f32),
            pltpu.VMEM((8 * (node_tiles - 1), LANES), f32),
            pltpu.VMEM((2 * reach + 1, 8 * (node_tiles - 1), LANES), f32),
            pltpu.VMEM(((2 * reach + 1) * leaves, 8, LANES), f32),
            pltpu.VMEM((3, nodes, LANES), f32),
            pltpu.VMEM((3, 3, parent_local.shape[0], shell), f32),
            pltpu.VMEM((leaves, 3 * shell), f32),
            pltpu.VMEM((3, leaves, shell), f32),
            pltpu.VMEM((3, nodes, LANES), f32),
            pltpu.VMEM((D, rows_sent // 2, LANES), f32),
            pltpu.VMEM((D, rows_sent // 2, LANES), f32),
            dma((1,)),
            dma((2,)),
            dma((2,)),
            dma((3,)),
            dma((3,)),
            dma((2 * reach + 1,)),
            dma((2 * reach + 1,)),
            dma((1,)),
            dma((1,)),
            dma((len(operands),)),
        ],
        compiler_params=pltpu.CompilerParams(
            collective_id=0, has_side_effects=True, vmem_limit_bytes=56 * 2**20
        ),
    )(*operands, l2l_maps)
    return pl.pallas_call(
        final,
        out_shape=jax.ShapeDtypeStruct((fibers, unknowns), f32),
        in_specs=[vmem, vmem, vmem],
        out_specs=vmem,
        compiler_params=pltpu.CompilerParams(vmem_limit_bytes=8 * 2**20),
    )(at_nodes, tension.reshape(1, nodes), blocks)


def solution(mesh):
    in_specs = (
        P(None, ("aa", "ba")),
        P(None, ("aa", "ba")),
        P(("aa", "ba")),
        P(("aa", "ba")),
        P(("aa", "ba"), None, None),
        P(("aa", "ba"), None, None),
        P(),
        P(("aa", "ba")),
        P(("aa", "ba")),
        P(("aa", "ba"), None),
        P(("aa", "ba"), None, None),
    )
    out_specs = P(("aa", "ba"), None)
    return jax.shard_map(local, mesh=mesh, in_specs=in_specs, out_specs=out_specs, check_vma=False)
```

```python
import functools

import jax
import jax.numpy as jnp
import numpy as np
from jax import lax
from jax.experimental import pallas as pl
from jax.experimental.pallas import tpu as pltpu
from jax.sharding import PartitionSpec as P

MOST = 4
NEAR_SPAN = 128

softening = 0.05
box_margin = 0.05
shell_radius = 2.95
golden_angle = 2.399963229728653
eight_pi = 25.132741228718345
LANES = 128
MESH = pl.DeviceIdType.MESH
f32, bf16, i32 = jnp.float32, jnp.bfloat16, jnp.int32


def surface(amount):
    indices = np.arange(amount, dtype=np.float32) + np.float32(0.5)
    height = np.float32(1.0) - np.float32(2.0) * indices / np.float32(amount)
    radius = np.sqrt(np.maximum(np.float32(1.0) - height * height, np.float32(0.0)))
    azimuth = indices * np.float32(golden_angle)
    spread = np.stack([radius * np.cos(azimuth), radius * np.sin(azimuth), height])
    return jnp.asarray(spread / np.max(np.abs(spread), axis=0, keepdims=True))


def split3_parts(x):
    high = x.astype(bf16).astype(f32)
    rest = x - high
    middle = rest.astype(bf16).astype(f32)
    return [high, middle, rest - middle]


def joined(r):
    n = r.shape[0] // 3
    return r[0:n] + (r[n : 2 * n] + r[2 * n : 3 * n])


def dot_t(a, b):
    return lax.dot_general(a, b, (((1,), (1,)), ((), ())), preferred_element_type=f32)


def dot_n(a, b):
    return lax.dot_general(a, b, (((1,), (0,)), ((), ())), preferred_element_type=f32)


def lane_sums(x):
    ones = jnp.ones((8, 2 * x.shape[1]), bf16)
    high = x.astype(bf16)
    low = (x - high.astype(f32)).astype(bf16)
    return dot_t(ones, jnp.concatenate([high, low], axis=1))


def hot(condition):
    return jnp.where(condition, 1.0, 0.0).astype(bf16)


def body(
    dims,
    fetches,
    slot_ref,
    pos_ref,
    frc_ref,
    lloc_ref,
    par_ref,
    lpar_ref,
    loct_ref,
    near_ref,
    shell_ref,
    maps_hbm,
    out_ref,
    maps_v,
    rank_hot,
    stage,
    flat,
    send,
    recv,
    mine,
    wide,
    rep,
    spots,
    parw,
    trans,
    dens,
    acc,
    rsend,
    rrecv,
    lane_at,
    tile_at_slot,
    local_sem,
    a_send,
    a_recv,
    p_send,
    p_recv,
    h_send,
    h_recv,
    r_send,
    r_recv,
):
    major, minor, reach = dims
    D = major * minor
    nodes = slot_ref.shape[1]
    cap = MOST * (nodes // D)
    per = LANES // cap
    tiles = D * cap // LANES
    slots = D * cap
    leaves = lloc_ref.shape[1]
    points = nodes // leaves
    node_tiles = nodes // LANES
    in_tile = LANES // points
    near_count = near_ref.shape[1]
    n_par = par_ref.shape[1]
    folds, rows_sent = send_form(cap)
    me = lax.axis_index("aa") * minor + lax.axis_index("ba")

    def dev(t):
        return (lax.div(t, minor), lax.rem(t, minor))

    def partner(k):
        return me ^ (D - k)

    maps_copy = pltpu.make_async_copy(maps_hbm, maps_v, local_sem.at[0])
    barrier = pltpu.get_barrier_semaphore()
    for fetch in fetches[0:3]:
        fetch.start()

    @pl.loop(1, D)
    def _(k):
        pl.semaphore_signal(
            barrier, inc=1, device_id=dev(partner(k)), device_id_type=MESH
        )

    for fetch in fetches[3:]:
        fetch.start()
    maps_copy.start()
    for fetch in fetches[0:3]:
        fetch.wait()

    def owner_of(slot):
        return jnp.floor((slot + 0.5) * (1.0 / nodes))

    def rows_of(shape, group=1):
        row = lax.broadcasted_iota(i32, shape, 0)
        return (row // group if group > 1 else row).astype(f32)

    slot_f = slot_ref[...].astype(f32)
    owner = owner_of(slot_f)
    within = slot_f - owner * nodes
    tile_at = jnp.floor((within + 0.5) * (1.0 / LANES))
    stage[0:3, :] = pos_ref[...]
    stage[3:6, :] = frc_ref[...]
    stage[6:7, :] = within - tile_at * LANES + 1.0
    stage[7:8, :] = tile_at

    owns = jnp.where(rows_of((D, nodes)) == owner, 1.0, 0.0)
    by_tile = [owns[:, t * LANES : (t + 1) * LANES] for t in range(node_tiles)]
    square = (LANES, 2 * LANES)
    over = lax.broadcasted_iota(i32, square, 1)
    before = hot((lax.broadcasted_iota(i32, square, 0) < over) | (over >= LANES))
    counts = dot_n(jnp.concatenate(by_tile, axis=0).astype(bf16), before)
    ranks, base = [], jnp.zeros((D, LANES), f32)
    for t in range(node_tiles):
        at = slice(t * D, (t + 1) * D)
        ranks.append(
            jnp.sum(by_tile[t] * (counts[at, 0:LANES] + base), axis=0, keepdims=True)
        )
        base = base + counts[at, LANES : 2 * LANES]
    rank = jnp.concatenate(ranks, axis=1)
    lane_ids = rows_of((LANES, nodes))
    for g in range(per):
        rank_hot[g] = hot(lane_ids == rank + float(g * cap))

    pieces = split3_parts(stage[...])
    sent = D * rows_sent
    mask = hot(rows_of((sent, nodes), rows_sent) == owner)
    lhs = []
    for piece in pieces:
        folded = []
        for h in range(folds):
            rows = piece[h * rows_sent : (h + 1) * rows_sent]
            rows = jnp.concatenate([rows] * (16 // rows_sent), axis=0).astype(bf16)
            folded.append(
                jnp.concatenate(
                    [mask[b : b + 16] * rows for b in range(0, sent, 16)], axis=0
                )
            )
        lhs.append(jnp.concatenate(folded, axis=1) if folds > 1 else folded[0])
    places = [rank_hot[h] for h in range(folds)]
    packed = joined(
        dot_t(
            jnp.concatenate(lhs, axis=0),
            jnp.concatenate(places, axis=1) if folds > 1 else places[0],
        )
    )
    for o in range(D):
        send[o] = packed[o * rows_sent : (o + 1) * rows_sent]

    pl.semaphore_wait(barrier, D - 1)

    def a2a(src, dst, s_sem, r_sem, group, to, index):
        return pltpu.make_async_remote_copy(
            src_ref=src.at[index],
            dst_ref=dst.at[me],
            send_sem=s_sem.at[group],
            recv_sem=r_sem.at[group],
            device_id=dev(to),
            device_id_type=MESH,
        )

    def all_of(dst, s_sem, r_sem, group, amount):
        whole = dst.at[pl.ds(0, amount)]
        return pltpu.make_async_remote_copy(
            src_ref=whole,
            dst_ref=whole,
            send_sem=s_sem.at[group],
            recv_sem=r_sem.at[group],
            device_id=dev(lax.rem(me + 1, D)),
            device_id_type=MESH,
        )

    @pl.loop(1, D)
    def _(k):
        to = partner(k)
        a2a(send, recv, a_send, a_recv, 0, to, to).start()

    def par_copy(step):
        return pltpu.make_async_remote_copy(
            src_ref=par_ref,
            dst_ref=parw.at[1 - step],
            send_sem=p_send.at[1 - step],
            recv_sem=p_recv.at[1 - step],
            device_id=dev(lax.rem(me + D + step, D)),
            device_id_type=MESH,
        )

    for fetch in fetches[3:]:
        fetch.wait()
    par_copy(1).start()
    par_copy(-1).start()
    recv[me] = send[me]
    parw[1] = par_ref[...]

    half_lanes = lax.broadcasted_iota(i32, (4, LANES), 1) < cap
    all_of(recv, a_send, a_recv, 0, D - 1).wait_recv()

    for t in range(tiles):
        at = slice(t * LANES, (t + 1) * LANES)
        if folds == 2:
            a, b = recv[2 * t], recv[2 * t + 1]
            flat[0:4, at] = jnp.where(half_lanes, a, pltpu.roll(b, cap, 1))
            flat[4:8, at] = jnp.where(half_lanes, pltpu.roll(a, cap, 1), b)
        else:
            total = recv[t * per]
            for g in range(1, per):
                total = total + pltpu.roll(recv[t * per + g], g * cap, 1)
            flat[:, at] = total
    arrived = split3_parts(flat[...])
    lane_hot = hot(rows_of((LANES, slots)) + 1.0 == flat[6:7, :])
    tile_row = flat[7:8, :]
    masked = [
        jnp.where(tile_row == float(t), part, 0.0)
        for t in range(node_tiles)
        for part in arrived
    ]
    placed = dot_t(jnp.concatenate(masked, axis=0).astype(bf16), lane_hot)
    unit = jnp.where(
        lax.broadcasted_iota(i32, (8, LANES), 0) < 3, 1.0 / softening, 1.0
    )
    placed_tiles = [joined(placed[24 * t : 24 * t + 24]) * unit for t in range(node_tiles)]
    last = placed_tiles[-1]
    for t in range(node_tiles - 1):
        mine[8 * t : 8 * t + 6, :] = placed_tiles[t][0:6]
        mine[8 * t + 6 : 8 * t + 8, :] = last[2 * t : 2 * t + 2]

    def halo(k, act):
        there = me - k if act == "wait_recv" else me + k

        @pl.when((there >= 0) & (there < D))
        def _():
            copy = pltpu.make_async_remote_copy(
                src_ref=mine,
                dst_ref=wide.at[reach - k],
                send_sem=h_send.at[reach - k],
                recv_sem=h_recv.at[reach - k],
                device_id=dev(there),
                device_id_type=MESH,
            )
            getattr(copy, act)()

    for k in sorted(range(1, reach + 1), key=lambda k: (abs(2 * k - reach), -k)):
        halo(k, "start")
        halo(-k, "start")

    wide[reach] = mine[...]
    for t in range(node_tiles):
        turned = jnp.transpose(placed_tiles[t])
        at = slice(t * LANES, (t + 1) * LANES)
        for c in range(3):
            spots[c, at, :] = jnp.broadcast_to(turned[:, c : c + 1], (LANES, LANES))

    par_copy(1).wait()
    par_copy(-1).wait()
    diagonal_of = (leaves, leaves)
    diagonal = lax.broadcasted_iota(i32, diagonal_of, 0) == lax.broadcasted_iota(
        i32, diagonal_of, 1
    )

    def column(row):
        return jnp.sum(jnp.where(diagonal, row.astype(f32), 0.0), axis=1, keepdims=True)

    wanted = column(lpar_ref[...] - (me - 1) * n_par)
    parts = []
    for c in range(3):
        total = jnp.zeros((leaves, LANES), f32)
        for j in range(3 * n_par):
            row = parw[j // n_par, c, j % n_par : j % n_par + 1, :]
            total = jnp.where(wanted == j, row, total)
        parts.append(total)
    wide_row = jnp.concatenate(parts, axis=1)
    high = wide_row.astype(bf16)
    low = (wide_row - high.astype(f32)).astype(bf16)
    both = jnp.concatenate([high, low], axis=0)
    octant = column(loct_ref[...])

    stage[3:4, :] = jnp.zeros((1, nodes), f32)
    for t in range(tiles):
        at = slice(t * LANES, (t + 1) * LANES)
        lane = jnp.maximum(flat[6:7, at] - 1.0, 0.0).astype(i32)
        lane_at[t] = jnp.broadcast_to(lane, (8, LANES))
        tile_at_slot[t] = jnp.broadcast_to(flat[7:8, at], (8, LANES))

    maps_copy.wait()
    trans[...] = jnp.zeros(trans.shape, f32)

    @pl.loop(0, maps_v.shape[0])
    def _(o):
        m = maps_v[o]
        m_high = m.astype(bf16)
        m_low = (m - m_high.astype(f32)).astype(bf16)
        first = dot_t(both, m_high)
        image = first[0:leaves] + (first[leaves : 2 * leaves] + dot_t(high, m_low))
        trans[...] = jnp.where(octant == jnp.asarray(o, i32).astype(f32), image, trans[...])

    for c in range(3):
        dens[c] = lloc_ref[c] + trans[:, c * LANES : (c + 1) * LANES]

    def pair_sums(targets, gaps_from, strengths, soft_by, sums):
        gap = [targets[c] - gaps_from[c] for c in range(3)]
        d2 = gap[0] * gap[0] + gap[1] * gap[1] + gap[2] * gap[2]
        soft = d2 + 1.0 if soft_by else d2
        inverse = lax.rsqrt(soft)
        weight = inverse * inverse * inverse
        along = gap[0] * strengths[0] + gap[1] * strengths[1] + gap[2] * strengths[2]
        near = inverse + weight if soft_by else inverse
        along = along * weight
        return [sums[c] + (near * strengths[c] + along * gap[c]) for c in range(3)]

    def leaf_rows(leaf):
        return pl.ds(pl.multiple_of(leaf * points, points), points)

    @pl.loop(0, leaves)
    def _(leaf):
        at = leaf_rows(leaf)
        targets = [spots[c, at, :] for c in range(3)]
        center = [jnp.sum(x, axis=0, keepdims=True) * (1.0 / points) for x in targets]
        spread = [
            jnp.max(jnp.abs(targets[c] - center[c]), axis=0, keepdims=True) for c in range(3)
        ]
        half = jnp.maximum(jnp.maximum(spread[0], spread[1]), spread[2])
        half = half + box_margin / softening
        points_at = [
            center[c] + shell_radius * half * shell_ref[c : c + 1, :] for c in range(3)
        ]
        density = [dens[c, pl.ds(leaf, 1), :] for c in range(3)]
        zero = jnp.zeros((points, LANES), f32)
        sums = pair_sums(targets, points_at, density, False, [zero, zero, zero])
        for c in range(3):
            acc[c, at, :] = sums[c]

    lane_group = lax.broadcasted_iota(i32, (8, LANES), 1) // points

    def spread_out(j):
        for t in range(node_tiles):
            if t < node_tiles - 1:
                tile = wide[j, 8 * t : 8 * t + 8, :]
            else:
                ends = [wide[j, 8 * i + 6 : 8 * i + 8, :] for i in range(node_tiles - 1)]
                tile = jnp.concatenate(ends + ends[0:1], axis=0)
            turned = [tile] + [pltpu.roll(tile, s * points, 1) for s in range(1, in_tile)]
            for i in range(in_tile):
                full = turned[(-i) % in_tile]
                for g in range(1, in_tile):
                    full = jnp.where(lane_group == g, turned[(g - i) % in_tile], full)
                rep[j * leaves + t * in_tile + i] = full

    spread_out(reach)
    together = 4 if reach % 4 == 0 else 1

    @pl.loop(0, reach // together)
    def _(step):
        ks = [step * together + 1 + i for i in range(together)]
        for k in ks:
            halo(k, "wait_recv")
            halo(-k, "wait_recv")
        for k in ks:
            spread_out(reach - k)
            spread_out(reach + k)

    first_leaf = (me - reach) * leaves

    def table_row(leaf, n):
        row = near_ref[leaf, n] - first_leaf
        return jnp.minimum(jnp.maximum(row, 0), rep.shape[0] - 1)

    def near_field(leaf):
        at = leaf_rows(leaf)
        targets = [spots[c, at, :] for c in range(3)]
        sums = [acc[c, at, :] for c in range(3)]
        for base in range(0, near_count, in_tile):
            count = min(in_tile, near_count - base)
            source = rep[table_row(leaf, base)]
            for g in range(1, count):
                source = jnp.where(lane_group == g, rep[table_row(leaf, base + g)], source)
            if count < in_tile:
                row = lax.broadcasted_iota(i32, (8, LANES), 0)
                source = jnp.where((lane_group >= count) & (row >= 3), 0.0, source)
            sums = pair_sums(
                targets,
                [source[c : c + 1] for c in range(3)],
                [source[c + 3 : c + 4] for c in range(3)],
                True,
                sums,
            )
        for c in range(3):
            acc[c, at, :] = sums[c]

    def row_sums(t):
        at = pl.ds(pl.multiple_of(t * LANES, LANES), LANES)
        for row, c in ((0, 0), (1, 2), (2, 1)):
            speed = jnp.sum(jnp.transpose(acc[c, at, :]), axis=0, keepdims=True)
            stage[row : row + 1, at] = speed * (1.0 / (eight_pi * softening))

    @pl.loop(0, node_tiles)
    def _(t):
        row_sums(jnp.maximum(t - 1, 0))
        for i in range(in_tile):
            near_field(t * in_tile + i)

    row_sums(node_tiles - 1)
    pairs = [
        jnp.concatenate(
            [stage[0:4, t * LANES : (t + 1) * LANES] for t in range(p, p + 2)], axis=0
        )
        for p in range(0, node_tiles, 2)
    ]
    for t in range(tiles):
        at = slice(t * LANES, (t + 1) * LANES)
        lane, tile = lane_at[t], tile_at_slot[t]
        found = jnp.take_along_axis(pairs[0], lane, axis=1)
        for p in range(1, len(pairs)):
            more = jnp.take_along_axis(pairs[p], lane, axis=1)
            found = jnp.where(tile >= float(2 * p), more, found)
        even = tile - jnp.floor(tile * 0.5) * 2.0
        found = jnp.where(even[0:4] > 0.5, found[4:8], found[0:4])
        if folds == 2:
            turned = pltpu.roll(found, cap, 1)
            left = half_lanes[0:2]
            rsend[2 * t] = jnp.where(left, found[0:2], turned[2:4])
            rsend[2 * t + 1] = jnp.where(left, turned[0:2], found[2:4])
        else:
            for g in range(per):
                rsend[t * per + g] = pltpu.roll(found, (LANES - g * cap) % LANES, 1)

    @pl.loop(1, D)
    def _(k):
        to = partner(k)
        a2a(rsend, rrecv, r_send, r_recv, 0, to, to).start()

    rrecv[me] = rsend[me]

    all_of(recv, a_send, a_recv, 0, D - 1).wait_send()

    @pl.loop(1, reach + 1)
    def _(k):
        halo(k, "wait_send")
        halo(-k, "wait_send")

    all_of(rrecv, r_send, r_recv, 0, D - 1).wait_recv()

    got = jnp.concatenate([rrecv[o] for o in range(D)], axis=0)
    got_high = got.astype(bf16)
    got_low = (got - got_high.astype(f32)).astype(bf16)
    sides = [rank_hot[h] for h in range(folds)]
    found = dot_n(
        jnp.concatenate([got_high, got_low], axis=0),
        jnp.concatenate(sides, axis=1) if folds > 1 else sides[0],
    )
    back = 4 // folds
    owner = owner_of(slot_ref[...].astype(f32))
    owner = jnp.concatenate([owner] * folds, axis=1)
    owner_rows = rows_of((8, folds * nodes), back)
    total = jnp.zeros((8, folds * nodes), f32)
    for b in range(0, D * back, 8):
        both_rows = found[b : b + 8] + found[D * back + b : D * back + b + 8]
        total = jnp.where(owner_rows + float(b // back) == owner, both_rows, total)
    while total.shape[0] > back:
        middle = total.shape[0] // 2
        total = total[0:middle] + total[middle:]
    out_ref[0:back, :] = total[:, 0:nodes]
    if folds > 1:
        out_ref[back : 2 * back, :] = total[:, nodes:]

    all_of(rrecv, r_send, r_recv, 0, D - 1).wait_send()


def final(nodes_ref, ten_ref, blocks_v, out_ref):
    at_nodes = nodes_ref[...]
    fibers = blocks_v.shape[0]
    npf = at_nodes.shape[1] // fibers
    per_tile = LANES // npf
    left = lax.broadcasted_iota(i32, (1, LANES), 1) < npf
    for i in range(fibers):
        t, g = i // per_tile, i % per_tile
        lanes = slice(t * LANES, (t + 1) * LANES)
        x, z, y = (at_nodes[c : c + 1, lanes] for c in range(3))
        tension = ten_ref[0:1, lanes]

        def side(v, to):
            turn = ((to - g) * npf) % LANES
            return pltpu.roll(v, turn, 1) if turn else v

        first = jnp.where(left, side(x, 0), side(y, 1))
        second = jnp.where(left, side(z, 0), side(tension, 1))
        products = blocks_v[i, :, 0:LANES] * first + blocks_v[i, :, LANES : 2 * LANES] * second
        half = products.shape[0] // 2
        out_ref[i : i + 1, half:] = lane_sums(products[half:])[0:1]
        turned = jnp.transpose(products[0:half])
        out_ref[i : i + 1, 0:half] = jnp.sum(turned, axis=0, keepdims=True)


def send_form(cap):
    folds = 2 if LANES == 2 * cap else 1
    return folds, 8 // folds


def kernel(dims, count, *refs):
    given, held = refs[0:count], refs[count + 2 : 2 * count + 2]
    fetch_sem = refs[-1]
    fetches = [
        pltpu.make_async_copy(given[n], held[n], fetch_sem.at[n]) for n in range(count)
    ]
    body(dims, fetches, *held, *refs[count : count + 2], *refs[2 * count + 2 : -1])


def local(
    positions,
    forces,
    tension,
    node_slot,
    leaf_local,
    parent_local,
    l2l_maps,
    leaf_parent,
    leaf_octant,
    near_list,
    blocks,
):
    major, minor = lax.axis_size("aa"), lax.axis_size("ba")
    D = major * minor
    nodes = node_slot.shape[0]
    leaves, _, shell = leaf_local.shape
    reach = -(-NEAR_SPAN // leaves)
    cap = MOST * (nodes // D)
    slots = D * cap
    fibers, unknowns, _ = blocks.shape
    node_tiles = nodes // LANES
    _, rows_sent = send_form(cap)
    vmem = pl.BlockSpec(memory_space=pltpu.VMEM)
    anywhere = pl.BlockSpec(memory_space=pl.ANY)
    dma = pltpu.SemaphoreType.DMA
    operands = (
        node_slot.reshape(1, nodes),
        positions,
        forces,
        leaf_local.transpose(1, 0, 2),
        parent_local.transpose(1, 0, 2),
        leaf_parent.reshape(1, leaves),
        leaf_octant.reshape(1, leaves),
        near_list,
        surface(shell),
    )
    held = [
        (pltpu.SMEM if x is near_list else pltpu.VMEM)(x.shape, x.dtype) for x in operands
    ]
    at_nodes = pl.pallas_call(
        functools.partial(kernel, (major, minor, reach), len(operands)),
        out_shape=pltpu.VMEM((4, nodes), f32),
        in_specs=[anywhere] * (len(operands) + 1),
        out_specs=vmem,
        scratch_shapes=held
        + [
            pltpu.VMEM(l2l_maps.shape, f32),
            pltpu.VMEM((LANES // cap, LANES, nodes), bf16),
            pltpu.VMEM((8, nodes), f32),
            pltpu.VMEM((8, slots), f32),
            pltpu.VMEM((D, rows_sent, LANES), f32),
            pltpu.VMEM((D, rows_sent, LANES), f32),
            pltpu.VMEM((8 * (node_tiles - 1), LANES), f32),
            pltpu.VMEM((2 * reach + 1, 8 * (node_tiles - 1), LANES), f32),
            pltpu.VMEM(((2 * reach + 1) * leaves, 8, LANES), f32),
            pltpu.VMEM((3, nodes, LANES), f32),
            pltpu.VMEM((3, 3, parent_local.shape[0], shell), f32),
            pltpu.VMEM((leaves, 3 * shell), f32),
            pltpu.VMEM((3, leaves, shell), f32),
            pltpu.VMEM((3, nodes, LANES), f32),
            pltpu.VMEM((D, rows_sent // 2, LANES), f32),
            pltpu.VMEM((D, rows_sent // 2, LANES), f32),
            pltpu.VMEM((slots // LANES, 8, LANES), i32),
            pltpu.VMEM((slots // LANES, 8, LANES), f32),
            dma((1,)),
            dma((2,)),
            dma((2,)),
            dma((3,)),
            dma((3,)),
            dma((2 * reach + 1,)),
            dma((2 * reach + 1,)),
            dma((1,)),
            dma((1,)),
            dma((len(operands),)),
        ],
        compiler_params=pltpu.CompilerParams(
            collective_id=0, has_side_effects=True, vmem_limit_bytes=56 * 2**20
        ),
    )(*operands, l2l_maps)
    return pl.pallas_call(
        final,
        out_shape=jax.ShapeDtypeStruct((fibers, unknowns), f32),
        in_specs=[vmem, vmem, vmem],
        out_specs=vmem,
        compiler_params=pltpu.CompilerParams(vmem_limit_bytes=8 * 2**20),
    )(at_nodes, tension.reshape(1, nodes), blocks)


def solution(mesh):
    in_specs = (
        P(None, ("aa", "ba")),
        P(None, ("aa", "ba")),
        P(("aa", "ba")),
        P(("aa", "ba")),
        P(("aa", "ba"), None, None),
        P(("aa", "ba"), None, None),
        P(),
        P(("aa", "ba")),
        P(("aa", "ba")),
        P(("aa", "ba"), None),
        P(("aa", "ba"), None, None),
    )
    out_specs = P(("aa", "ba"), None)
    return jax.shard_map(local, mesh=mesh, in_specs=in_specs, out_specs=out_specs, check_vma=False)
```

```python
import functools

import jax
import jax.numpy as jnp
import numpy as np
from jax import lax
from jax.experimental import pallas as pl
from jax.experimental.pallas import tpu as pltpu
from jax.sharding import PartitionSpec as P

MOST = 4
NEAR_SPAN = 128

softening = 0.05
box_margin = 0.05
shell_radius = 2.95
golden_angle = 2.399963229728653
eight_pi = 25.132741228718345
LANES = 128
MESH = pl.DeviceIdType.MESH
f32, bf16, i32 = jnp.float32, jnp.bfloat16, jnp.int32


def surface(amount):
    indices = np.arange(amount, dtype=np.float32) + np.float32(0.5)
    height = np.float32(1.0) - np.float32(2.0) * indices / np.float32(amount)
    radius = np.sqrt(np.maximum(np.float32(1.0) - height * height, np.float32(0.0)))
    azimuth = indices * np.float32(golden_angle)
    spread = np.stack([radius * np.cos(azimuth), radius * np.sin(azimuth), height])
    return jnp.asarray(spread / np.max(np.abs(spread), axis=0, keepdims=True))


def split3_parts(x):
    high = x.astype(bf16).astype(f32)
    rest = x - high
    middle = rest.astype(bf16).astype(f32)
    return [high, middle, rest - middle]


def joined(r):
    n = r.shape[0] // 3
    return r[0:n] + (r[n : 2 * n] + r[2 * n : 3 * n])


def dot_t(a, b):
    return lax.dot_general(a, b, (((1,), (1,)), ((), ())), preferred_element_type=f32)


def dot_n(a, b):
    return lax.dot_general(a, b, (((1,), (0,)), ((), ())), preferred_element_type=f32)


def lane_sums(x):
    ones = jnp.ones((8, 2 * x.shape[1]), bf16)
    high = x.astype(bf16)
    low = (x - high.astype(f32)).astype(bf16)
    return dot_t(ones, jnp.concatenate([high, low], axis=1))


def hot(condition):
    return jnp.where(condition, 1.0, 0.0).astype(bf16)


def body(
    dims,
    fetches,
    slot_ref,
    pos_ref,
    frc_ref,
    lloc_ref,
    par_ref,
    lpar_ref,
    loct_ref,
    near_ref,
    shell_ref,
    maps_hbm,
    out_ref,
    maps_v,
    rank_hot,
    stage,
    flat,
    send,
    recv,
    mine,
    wide,
    rep,
    spots,
    parw,
    trans,
    dens,
    acc,
    rsend,
    rrecv,
    lane_at,
    tile_at_slot,
    local_sem,
    a_send,
    a_recv,
    p_send,
    p_recv,
    h_send,
    h_recv,
    r_send,
    r_recv,
):
    major, minor, reach = dims
    D = major * minor
    nodes = slot_ref.shape[1]
    cap = MOST * (nodes // D)
    per = LANES // cap
    tiles = D * cap // LANES
    slots = D * cap
    leaves = lloc_ref.shape[1]
    points = nodes // leaves
    node_tiles = nodes // LANES
    in_tile = LANES // points
    near_count = near_ref.shape[1]
    n_par = par_ref.shape[1]
    folds, rows_sent = send_form(cap)
    me = lax.axis_index("aa") * minor + lax.axis_index("ba")

    def dev(t):
        return (lax.div(t, minor), lax.rem(t, minor))

    def partner(k):
        return me ^ (D - k)

    maps_copy = pltpu.make_async_copy(maps_hbm, maps_v, local_sem.at[0])
    barrier = pltpu.get_barrier_semaphore()
    for fetch in fetches[0:3]:
        fetch.start()

    @pl.loop(1, D)
    def _(k):
        pl.semaphore_signal(
            barrier, inc=1, device_id=dev(partner(k)), device_id_type=MESH
        )

    for fetch in fetches[3:]:
        fetch.start()
    maps_copy.start()
    for fetch in fetches[0:3]:
        fetch.wait()

    def owner_of(slot):
        return jnp.floor((slot + 0.5) * (1.0 / nodes))

    def rows_of(shape, group=1):
        row = lax.broadcasted_iota(i32, shape, 0)
        return (row // group if group > 1 else row).astype(f32)

    slot_f = slot_ref[...].astype(f32)
    owner = owner_of(slot_f)
    within = slot_f - owner * nodes
    tile_at = jnp.floor((within + 0.5) * (1.0 / LANES))
    stage[0:3, :] = pos_ref[...]
    stage[3:6, :] = frc_ref[...]
    stage[6:7, :] = within - tile_at * LANES + 1.0
    stage[7:8, :] = tile_at

    owns = jnp.where(rows_of((D, nodes)) == owner, 1.0, 0.0)
    by_tile = [owns[:, t * LANES : (t + 1) * LANES] for t in range(node_tiles)]
    square = (LANES, 2 * LANES)
    over = lax.broadcasted_iota(i32, square, 1)
    before = hot((lax.broadcasted_iota(i32, square, 0) < over) | (over >= LANES))
    counts = dot_n(jnp.concatenate(by_tile, axis=0).astype(bf16), before)
    ranks, base = [], jnp.zeros((D, LANES), f32)
    for t in range(node_tiles):
        at = slice(t * D, (t + 1) * D)
        ranks.append(
            jnp.sum(by_tile[t] * (counts[at, 0:LANES] + base), axis=0, keepdims=True)
        )
        base = base + counts[at, LANES : 2 * LANES]
    rank = jnp.concatenate(ranks, axis=1)
    lane_ids = rows_of((LANES, nodes))
    for g in range(per):
        rank_hot[g] = hot(lane_ids == rank + float(g * cap))

    pieces = split3_parts(stage[...])
    sent = D * rows_sent
    mask = hot(rows_of((sent, nodes), rows_sent) == owner)
    lhs = []
    for piece in pieces:
        folded = []
        for h in range(folds):
            rows = piece[h * rows_sent : (h + 1) * rows_sent]
            rows = jnp.concatenate([rows] * (16 // rows_sent), axis=0).astype(bf16)
            folded.append(
                jnp.concatenate(
                    [mask[b : b + 16] * rows for b in range(0, sent, 16)], axis=0
                )
            )
        lhs.append(jnp.concatenate(folded, axis=1) if folds > 1 else folded[0])
    places = [rank_hot[h] for h in range(folds)]
    packed = joined(
        dot_t(
            jnp.concatenate(lhs, axis=0),
            jnp.concatenate(places, axis=1) if folds > 1 else places[0],
        )
    )
    for o in range(D):
        send[o] = packed[o * rows_sent : (o + 1) * rows_sent]

    pl.semaphore_wait(barrier, D - 1)

    def a2a(src, dst, s_sem, r_sem, group, to, index):
        return pltpu.make_async_remote_copy(
            src_ref=src.at[index],
            dst_ref=dst.at[me],
            send_sem=s_sem.at[group],
            recv_sem=r_sem.at[group],
            device_id=dev(to),
            device_id_type=MESH,
        )

    def all_of(dst, s_sem, r_sem, group, amount):
        whole = dst.at[pl.ds(0, amount)]
        return pltpu.make_async_remote_copy(
            src_ref=whole,
            dst_ref=whole,
            send_sem=s_sem.at[group],
            recv_sem=r_sem.at[group],
            device_id=dev(lax.rem(me + 1, D)),
            device_id_type=MESH,
        )

    @pl.loop(1, D)
    def _(k):
        to = partner(k)
        a2a(send, recv, a_send, a_recv, 0, to, to).start()

    def par_copy(step):
        return pltpu.make_async_remote_copy(
            src_ref=par_ref,
            dst_ref=parw.at[1 - step],
            send_sem=p_send.at[1 - step],
            recv_sem=p_recv.at[1 - step],
            device_id=dev(lax.rem(me + D + step, D)),
            device_id_type=MESH,
        )

    for fetch in fetches[3:]:
        fetch.wait()
    par_copy(1).start()
    par_copy(-1).start()
    recv[me] = send[me]
    parw[1] = par_ref[...]

    half_lanes = lax.broadcasted_iota(i32, (4, LANES), 1) < cap
    all_of(recv, a_send, a_recv, 0, D - 1).wait_recv()

    for t in range(tiles):
        at = slice(t * LANES, (t + 1) * LANES)
        if folds == 2:
            a, b = recv[2 * t], recv[2 * t + 1]
            flat[0:4, at] = jnp.where(half_lanes, a, pltpu.roll(b, cap, 1))
            flat[4:8, at] = jnp.where(half_lanes, pltpu.roll(a, cap, 1), b)
        else:
            total = recv[t * per]
            for g in range(1, per):
                total = total + pltpu.roll(recv[t * per + g], g * cap, 1)
            flat[:, at] = total
    arrived = split3_parts(flat[...])
    lane_hot = hot(rows_of((LANES, slots)) + 1.0 == flat[6:7, :])
    tile_row = flat[7:8, :]
    masked = [
        jnp.where(tile_row == float(t), part, 0.0)
        for t in range(node_tiles)
        for part in arrived
    ]
    placed = dot_t(jnp.concatenate(masked, axis=0).astype(bf16), lane_hot)
    unit = jnp.where(
        lax.broadcasted_iota(i32, (8, LANES), 0) < 3, 1.0 / softening, 1.0
    )
    placed_tiles = [joined(placed[24 * t : 24 * t + 24]) * unit for t in range(node_tiles)]
    last = placed_tiles[-1]
    for t in range(node_tiles - 1):
        mine[8 * t : 8 * t + 6, :] = placed_tiles[t][0:6]
        mine[8 * t + 6 : 8 * t + 8, :] = last[2 * t : 2 * t + 2]

    def halo(k, act):
        there = me - k if act == "wait_recv" else me + k

        @pl.when((there >= 0) & (there < D))
        def _():
            copy = pltpu.make_async_remote_copy(
                src_ref=mine,
                dst_ref=wide.at[reach - k],
                send_sem=h_send.at[reach - k],
                recv_sem=h_recv.at[reach - k],
                device_id=dev(there),
                device_id_type=MESH,
            )
            getattr(copy, act)()

    for k in sorted(range(1, reach + 1), key=lambda k: (abs(2 * k - reach), -k)):
        halo(k, "start")
        halo(-k, "start")

    wide[reach] = mine[...]
    for t in range(node_tiles):
        turned = jnp.transpose(placed_tiles[t])
        at = slice(t * LANES, (t + 1) * LANES)
        for c in range(3):
            spots[c, at, :] = jnp.broadcast_to(turned[:, c : c + 1], (LANES, LANES))

    par_copy(1).wait()
    par_copy(-1).wait()
    diagonal_of = (leaves, leaves)
    diagonal = lax.broadcasted_iota(i32, diagonal_of, 0) == lax.broadcasted_iota(
        i32, diagonal_of, 1
    )

    def column(row):
        return jnp.sum(jnp.where(diagonal, row.astype(f32), 0.0), axis=1, keepdims=True)

    wanted = column(lpar_ref[...] - (me - 1) * n_par)
    parts = []
    for c in range(3):
        total = jnp.zeros((leaves, LANES), f32)
        for j in range(3 * n_par):
            row = parw[j // n_par, c, j % n_par : j % n_par + 1, :]
            total = jnp.where(wanted == j, row, total)
        parts.append(total)
    wide_row = jnp.concatenate(parts, axis=1)
    high = wide_row.astype(bf16)
    low = (wide_row - high.astype(f32)).astype(bf16)
    both = jnp.concatenate([high, low], axis=0)
    octant = column(loct_ref[...])

    stage[3:4, :] = jnp.zeros((1, nodes), f32)
    for t in range(tiles):
        at = slice(t * LANES, (t + 1) * LANES)
        lane = jnp.maximum(flat[6:7, at] - 1.0, 0.0).astype(i32)
        lane_at[t] = jnp.broadcast_to(lane, (8, LANES))
        tile_at_slot[t] = jnp.broadcast_to(flat[7:8, at], (8, LANES))

    maps_copy.wait()
    trans[...] = jnp.zeros(trans.shape, f32)

    @pl.loop(0, maps_v.shape[0])
    def _(o):
        m = maps_v[o]
        m_high = m.astype(bf16)
        m_low = (m - m_high.astype(f32)).astype(bf16)
        first = dot_t(both, m_high)
        image = first[0:leaves] + (first[leaves : 2 * leaves] + dot_t(high, m_low))
        trans[...] = jnp.where(octant == jnp.asarray(o, i32).astype(f32), image, trans[...])

    for c in range(3):
        dens[c] = lloc_ref[c] + trans[:, c * LANES : (c + 1) * LANES]

    def pair_sums(targets, gaps_from, strengths, soft_by, sums):
        gap = [targets[c] - gaps_from[c] for c in range(3)]
        d2 = gap[0] * gap[0] + gap[1] * gap[1] + gap[2] * gap[2]
        soft = d2 + 1.0 if soft_by else d2
        inverse = lax.rsqrt(soft)
        weight = inverse * inverse * inverse
        along = gap[0] * strengths[0] + gap[1] * strengths[1] + gap[2] * strengths[2]
        near = inverse + weight if soft_by else inverse
        along = along * weight
        return [sums[c] + (near * strengths[c] + along * gap[c]) for c in range(3)]

    def leaf_rows(leaf):
        return pl.ds(pl.multiple_of(leaf * points, points), points)

    @pl.loop(0, leaves)
    def _(leaf):
        at = leaf_rows(leaf)
        targets = [spots[c, at, :] for c in range(3)]
        center = [jnp.sum(x, axis=0, keepdims=True) * (1.0 / points) for x in targets]
        spread = [
            jnp.max(jnp.abs(targets[c] - center[c]), axis=0, keepdims=True) for c in range(3)
        ]
        half = jnp.maximum(jnp.maximum(spread[0], spread[1]), spread[2])
        half = half + box_margin / softening
        points_at = [
            center[c] + shell_radius * half * shell_ref[c : c + 1, :] for c in range(3)
        ]
        density = [dens[c, pl.ds(leaf, 1), :] for c in range(3)]
        zero = jnp.zeros((points, LANES), f32)
        sums = pair_sums(targets, points_at, density, False, [zero, zero, zero])
        for c in range(3):
            acc[c, at, :] = sums[c]

    lane_group = lax.broadcasted_iota(i32, (8, LANES), 1) // points

    def spread_out(j):
        for t in range(node_tiles):
            if t < node_tiles - 1:
                tile = wide[j, 8 * t : 8 * t + 8, :]
            else:
                ends = [wide[j, 8 * i + 6 : 8 * i + 8, :] for i in range(node_tiles - 1)]
                tile = jnp.concatenate(ends + ends[0:1], axis=0)
            turned = [tile] + [pltpu.roll(tile, s * points, 1) for s in range(1, in_tile)]
            for i in range(in_tile):
                full = turned[(-i) % in_tile]
                for g in range(1, in_tile):
                    full = jnp.where(lane_group == g, turned[(g - i) % in_tile], full)
                rep[j * leaves + t * in_tile + i] = full

    spread_out(reach)
    together = reach

    @pl.loop(0, reach // together)
    def _(step):
        ks = [step * together + 1 + i for i in range(together)]
        for k in ks:
            halo(k, "wait_recv")
            halo(-k, "wait_recv")
        for k in ks:
            spread_out(reach - k)
            spread_out(reach + k)

    first_leaf = (me - reach) * leaves

    def table_row(leaf, n):
        row = near_ref[leaf, n] - first_leaf
        return jnp.minimum(jnp.maximum(row, 0), rep.shape[0] - 1)

    def near_field(leaf):
        at = leaf_rows(leaf)
        targets = [spots[c, at, :] for c in range(3)]
        sums = [acc[c, at, :] for c in range(3)]
        for base in range(0, near_count, in_tile):
            count = min(in_tile, near_count - base)
            source = rep[table_row(leaf, base)]
            for g in range(1, count):
                source = jnp.where(lane_group == g, rep[table_row(leaf, base + g)], source)
            if count < in_tile:
                row = lax.broadcasted_iota(i32, (8, LANES), 0)
                source = jnp.where((lane_group >= count) & (row >= 3), 0.0, source)
            sums = pair_sums(
                targets,
                [source[c : c + 1] for c in range(3)],
                [source[c + 3 : c + 4] for c in range(3)],
                True,
                sums,
            )
        for c in range(3):
            acc[c, at, :] = sums[c]

    def row_sums(t):
        at = pl.ds(pl.multiple_of(t * LANES, LANES), LANES)
        for row, c in ((0, 0), (1, 2), (2, 1)):
            speed = jnp.sum(jnp.transpose(acc[c, at, :]), axis=0, keepdims=True)
            stage[row : row + 1, at] = speed * (1.0 / (eight_pi * softening))

    @pl.loop(0, node_tiles)
    def _(t):
        row_sums(jnp.maximum(t - 1, 0))
        for i in range(in_tile):
            near_field(t * in_tile + i)

    row_sums(node_tiles - 1)
    pairs = [
        jnp.concatenate(
            [stage[0:4, t * LANES : (t + 1) * LANES] for t in range(p, p + 2)], axis=0
        )
        for p in range(0, node_tiles, 2)
    ]
    for t in range(tiles):
        at = slice(t * LANES, (t + 1) * LANES)
        lane, tile = lane_at[t], tile_at_slot[t]
        found = jnp.take_along_axis(pairs[0], lane, axis=1)
        for p in range(1, len(pairs)):
            more = jnp.take_along_axis(pairs[p], lane, axis=1)
            found = jnp.where(tile >= float(2 * p), more, found)
        even = tile - jnp.floor(tile * 0.5) * 2.0
        found = jnp.where(even[0:4] > 0.5, found[4:8], found[0:4])
        if folds == 2:
            turned = pltpu.roll(found, cap, 1)
            left = half_lanes[0:2]
            rsend[2 * t] = jnp.where(left, found[0:2], turned[2:4])
            rsend[2 * t + 1] = jnp.where(left, turned[0:2], found[2:4])
        else:
            for g in range(per):
                rsend[t * per + g] = pltpu.roll(found, (LANES - g * cap) % LANES, 1)

    @pl.loop(1, D)
    def _(k):
        to = partner(k)
        a2a(rsend, rrecv, r_send, r_recv, 0, to, to).start()

    rrecv[me] = rsend[me]

    all_of(recv, a_send, a_recv, 0, D - 1).wait_send()

    @pl.loop(1, reach + 1)
    def _(k):
        halo(k, "wait_send")
        halo(-k, "wait_send")

    all_of(rrecv, r_send, r_recv, 0, D - 1).wait_recv()

    got = jnp.concatenate([rrecv[o] for o in range(D)], axis=0)
    got_high = got.astype(bf16)
    got_low = (got - got_high.astype(f32)).astype(bf16)
    sides = [rank_hot[h] for h in range(folds)]
    found = dot_n(
        jnp.concatenate([got_high, got_low], axis=0),
        jnp.concatenate(sides, axis=1) if folds > 1 else sides[0],
    )
    back = 4 // folds
    owner = owner_of(slot_ref[...].astype(f32))
    owner = jnp.concatenate([owner] * folds, axis=1)
    owner_rows = rows_of((8, folds * nodes), back)
    total = jnp.zeros((8, folds * nodes), f32)
    for b in range(0, D * back, 8):
        both_rows = found[b : b + 8] + found[D * back + b : D * back + b + 8]
        total = jnp.where(owner_rows + float(b // back) == owner, both_rows, total)
    while total.shape[0] > back:
        middle = total.shape[0] // 2
        total = total[0:middle] + total[middle:]
    out_ref[0:back, :] = total[:, 0:nodes]
    if folds > 1:
        out_ref[back : 2 * back, :] = total[:, nodes:]

    all_of(rrecv, r_send, r_recv, 0, D - 1).wait_send()


def final(nodes_ref, ten_ref, blocks_v, out_ref):
    at_nodes = nodes_ref[...]
    fibers = blocks_v.shape[0]
    npf = at_nodes.shape[1] // fibers
    per_tile = LANES // npf
    left = lax.broadcasted_iota(i32, (1, LANES), 1) < npf
    for i in range(fibers):
        t, g = i // per_tile, i % per_tile
        lanes = slice(t * LANES, (t + 1) * LANES)
        x, z, y = (at_nodes[c : c + 1, lanes] for c in range(3))
        tension = ten_ref[0:1, lanes]

        def side(v, to):
            turn = ((to - g) * npf) % LANES
            return pltpu.roll(v, turn, 1) if turn else v

        first = jnp.where(left, side(x, 0), side(y, 1))
        second = jnp.where(left, side(z, 0), side(tension, 1))
        products = blocks_v[i, :, 0:LANES] * first + blocks_v[i, :, LANES : 2 * LANES] * second
        half = products.shape[0] // 2
        out_ref[i : i + 1, half:] = lane_sums(products[half:])[0:1]
        turned = jnp.transpose(products[0:half])
        out_ref[i : i + 1, 0:half] = jnp.sum(turned, axis=0, keepdims=True)


def send_form(cap):
    folds = 2 if LANES == 2 * cap else 1
    return folds, 8 // folds


def kernel(dims, count, *refs):
    given, held = refs[0:count], refs[count + 2 : 2 * count + 2]
    fetch_sem = refs[-1]
    fetches = [
        pltpu.make_async_copy(given[n], held[n], fetch_sem.at[n]) for n in range(count)
    ]
    body(dims, fetches, *held, *refs[count : count + 2], *refs[2 * count + 2 : -1])


def local(
    positions,
    forces,
    tension,
    node_slot,
    leaf_local,
    parent_local,
    l2l_maps,
    leaf_parent,
    leaf_octant,
    near_list,
    blocks,
):
    major, minor = lax.axis_size("aa"), lax.axis_size("ba")
    D = major * minor
    nodes = node_slot.shape[0]
    leaves, _, shell = leaf_local.shape
    reach = -(-NEAR_SPAN // leaves)
    cap = MOST * (nodes // D)
    slots = D * cap
    fibers, unknowns, _ = blocks.shape
    node_tiles = nodes // LANES
    _, rows_sent = send_form(cap)
    vmem = pl.BlockSpec(memory_space=pltpu.VMEM)
    anywhere = pl.BlockSpec(memory_space=pl.ANY)
    dma = pltpu.SemaphoreType.DMA
    operands = (
        node_slot.reshape(1, nodes),
        positions,
        forces,
        leaf_local.transpose(1, 0, 2),
        parent_local.transpose(1, 0, 2),
        leaf_parent.reshape(1, leaves),
        leaf_octant.reshape(1, leaves),
        near_list,
        surface(shell),
    )
    held = [
        (pltpu.SMEM if x is near_list else pltpu.VMEM)(x.shape, x.dtype) for x in operands
    ]
    at_nodes = pl.pallas_call(
        functools.partial(kernel, (major, minor, reach), len(operands)),
        out_shape=pltpu.VMEM((4, nodes), f32),
        in_specs=[anywhere] * (len(operands) + 1),
        out_specs=vmem,
        scratch_shapes=held
        + [
            pltpu.VMEM(l2l_maps.shape, f32),
            pltpu.VMEM((LANES // cap, LANES, nodes), bf16),
            pltpu.VMEM((8, nodes), f32),
            pltpu.VMEM((8, slots), f32),
            pltpu.VMEM((D, rows_sent, LANES), f32),
            pltpu.VMEM((D, rows_sent, LANES), f32),
            pltpu.VMEM((8 * (node_tiles - 1), LANES), f32),
            pltpu.VMEM((2 * reach + 1, 8 * (node_tiles - 1), LANES), f32),
            pltpu.VMEM(((2 * reach + 1) * leaves, 8, LANES), f32),
            pltpu.VMEM((3, nodes, LANES), f32),
            pltpu.VMEM((3, 3, parent_local.shape[0], shell), f32),
            pltpu.VMEM((leaves, 3 * shell), f32),
            pltpu.VMEM((3, leaves, shell), f32),
            pltpu.VMEM((3, nodes, LANES), f32),
            pltpu.VMEM((D, rows_sent // 2, LANES), f32),
            pltpu.VMEM((D, rows_sent // 2, LANES), f32),
            pltpu.VMEM((slots // LANES, 8, LANES), i32),
            pltpu.VMEM((slots // LANES, 8, LANES), f32),
            dma((1,)),
            dma((2,)),
            dma((2,)),
            dma((3,)),
            dma((3,)),
            dma((2 * reach + 1,)),
            dma((2 * reach + 1,)),
            dma((1,)),
            dma((1,)),
            dma((len(operands),)),
        ],
        compiler_params=pltpu.CompilerParams(
            collective_id=0, has_side_effects=True, vmem_limit_bytes=56 * 2**20
        ),
    )(*operands, l2l_maps)
    return pl.pallas_call(
        final,
        out_shape=jax.ShapeDtypeStruct((fibers, unknowns), f32),
        in_specs=[vmem, vmem, vmem],
        out_specs=vmem,
        compiler_params=pltpu.CompilerParams(vmem_limit_bytes=8 * 2**20),
    )(at_nodes, tension.reshape(1, nodes), blocks)


def solution(mesh):
    in_specs = (
        P(None, ("aa", "ba")),
        P(None, ("aa", "ba")),
        P(("aa", "ba")),
        P(("aa", "ba")),
        P(("aa", "ba"), None, None),
        P(("aa", "ba"), None, None),
        P(),
        P(("aa", "ba")),
        P(("aa", "ba")),
        P(("aa", "ba"), None),
        P(("aa", "ba"), None, None),
    )
    out_specs = P(("aa", "ba"), None)
    return jax.shard_map(local, mesh=mesh, in_specs=in_specs, out_specs=out_specs, check_vma=False)
```

```python
import functools

import jax
import jax.numpy as jnp
import numpy as np
from jax import lax
from jax.experimental import pallas as pl
from jax.experimental.pallas import tpu as pltpu
from jax.sharding import PartitionSpec as P

MOST = 4
NEAR_SPAN = 128

softening = 0.05
box_margin = 0.05
shell_radius = 2.95
golden_angle = 2.399963229728653
eight_pi = 25.132741228718345
LANES = 128
MESH = pl.DeviceIdType.MESH
f32, bf16, i32 = jnp.float32, jnp.bfloat16, jnp.int32


def surface(amount):
    indices = np.arange(amount, dtype=np.float32) + np.float32(0.5)
    height = np.float32(1.0) - np.float32(2.0) * indices / np.float32(amount)
    radius = np.sqrt(np.maximum(np.float32(1.0) - height * height, np.float32(0.0)))
    azimuth = indices * np.float32(golden_angle)
    spread = np.stack([radius * np.cos(azimuth), radius * np.sin(azimuth), height])
    return jnp.asarray(spread / np.max(np.abs(spread), axis=0, keepdims=True))


def split3_parts(x):
    high = x.astype(bf16).astype(f32)
    rest = x - high
    middle = rest.astype(bf16).astype(f32)
    return [high, middle, rest - middle]


def joined(r):
    n = r.shape[0] // 3
    return r[0:n] + (r[n : 2 * n] + r[2 * n : 3 * n])


def dot_t(a, b):
    return lax.dot_general(a, b, (((1,), (1,)), ((), ())), preferred_element_type=f32)


def dot_n(a, b):
    return lax.dot_general(a, b, (((1,), (0,)), ((), ())), preferred_element_type=f32)


def lane_sums(x):
    ones = jnp.ones((8, 2 * x.shape[1]), bf16)
    high = x.astype(bf16)
    low = (x - high.astype(f32)).astype(bf16)
    return dot_t(ones, jnp.concatenate([high, low], axis=1))


def hot(condition):
    return jnp.where(condition, 1.0, 0.0).astype(bf16)


def body(
    dims,
    fetches,
    slot_ref,
    pos_ref,
    frc_ref,
    lloc_ref,
    par_ref,
    lpar_ref,
    loct_ref,
    near_ref,
    shell_ref,
    maps_hbm,
    out_ref,
    maps_v,
    rank_hot,
    stage,
    flat,
    send,
    recv,
    mine,
    wide,
    rep,
    spots,
    parw,
    trans,
    dens,
    acc,
    rsend,
    rrecv,
    lane_at,
    tile_at_slot,
    local_sem,
    a_send,
    a_recv,
    p_send,
    p_recv,
    h_send,
    h_recv,
    r_send,
    r_recv,
):
    major, minor, reach = dims
    D = major * minor
    nodes = slot_ref.shape[1]
    cap = MOST * (nodes // D)
    per = LANES // cap
    tiles = D * cap // LANES
    slots = D * cap
    leaves = lloc_ref.shape[1]
    points = nodes // leaves
    node_tiles = nodes // LANES
    in_tile = LANES // points
    near_count = near_ref.shape[1]
    n_par = par_ref.shape[1]
    folds, rows_sent = send_form(cap)
    me = lax.axis_index("aa") * minor + lax.axis_index("ba")

    def dev(t):
        return (lax.div(t, minor), lax.rem(t, minor))

    def partner(k):
        return me ^ (D - k)

    maps_copy = pltpu.make_async_copy(maps_hbm, maps_v, local_sem.at[0])
    barrier = pltpu.get_barrier_semaphore()
    for fetch in fetches[0:3]:
        fetch.start()

    @pl.loop(1, D)
    def _(k):
        pl.semaphore_signal(
            barrier, inc=1, device_id=dev(partner(k)), device_id_type=MESH
        )

    for fetch in fetches[3:]:
        fetch.start()
    maps_copy.start()
    for fetch in fetches[0:3]:
        fetch.wait()

    def owner_of(slot):
        return jnp.floor((slot + 0.5) * (1.0 / nodes))

    def rows_of(shape, group=1):
        row = lax.broadcasted_iota(i32, shape, 0)
        return (row // group if group > 1 else row).astype(f32)

    slot_f = slot_ref[...].astype(f32)
    owner = owner_of(slot_f)
    within = slot_f - owner * nodes
    tile_at = jnp.floor((within + 0.5) * (1.0 / LANES))
    stage[0:3, :] = pos_ref[...]
    stage[3:6, :] = frc_ref[...]
    stage[6:7, :] = within - tile_at * LANES + 1.0
    stage[7:8, :] = tile_at

    owns = jnp.where(rows_of((D, nodes)) == owner, 1.0, 0.0)
    by_tile = [owns[:, t * LANES : (t + 1) * LANES] for t in range(node_tiles)]
    square = (LANES, 2 * LANES)
    over = lax.broadcasted_iota(i32, square, 1)
    before = hot((lax.broadcasted_iota(i32, square, 0) < over) | (over >= LANES))
    counts = dot_n(jnp.concatenate(by_tile, axis=0).astype(bf16), before)
    ranks, base = [], jnp.zeros((D, LANES), f32)
    for t in range(node_tiles):
        at = slice(t * D, (t + 1) * D)
        ranks.append(
            jnp.sum(by_tile[t] * (counts[at, 0:LANES] + base), axis=0, keepdims=True)
        )
        base = base + counts[at, LANES : 2 * LANES]
    rank = jnp.concatenate(ranks, axis=1)
    lane_ids = rows_of((LANES, nodes))
    for g in range(per):
        rank_hot[g] = hot(lane_ids == rank + float(g * cap))

    pieces = split3_parts(stage[...])
    sent = D * rows_sent
    mask = hot(rows_of((sent, nodes), rows_sent) == owner)
    lhs = []
    for piece in pieces:
        folded = []
        for h in range(folds):
            rows = piece[h * rows_sent : (h + 1) * rows_sent]
            rows = jnp.concatenate([rows] * (16 // rows_sent), axis=0).astype(bf16)
            folded.append(
                jnp.concatenate(
                    [mask[b : b + 16] * rows for b in range(0, sent, 16)], axis=0
                )
            )
        lhs.append(jnp.concatenate(folded, axis=1) if folds > 1 else folded[0])
    places = [rank_hot[h] for h in range(folds)]
    packed = joined(
        dot_t(
            jnp.concatenate(lhs, axis=0),
            jnp.concatenate(places, axis=1) if folds > 1 else places[0],
        )
    )
    for o in range(D):
        send[o] = packed[o * rows_sent : (o + 1) * rows_sent]

    pl.semaphore_wait(barrier, D - 1)

    def a2a(src, dst, s_sem, r_sem, group, to, index):
        return pltpu.make_async_remote_copy(
            src_ref=src.at[index],
            dst_ref=dst.at[me],
            send_sem=s_sem.at[group],
            recv_sem=r_sem.at[group],
            device_id=dev(to),
            device_id_type=MESH,
        )

    def all_of(dst, s_sem, r_sem, group, amount):
        whole = dst.at[pl.ds(0, amount)]
        return pltpu.make_async_remote_copy(
            src_ref=whole,
            dst_ref=whole,
            send_sem=s_sem.at[group],
            recv_sem=r_sem.at[group],
            device_id=dev(lax.rem(me + 1, D)),
            device_id_type=MESH,
        )

    @pl.loop(1, D)
    def _(k):
        to = partner(k)
        a2a(send, recv, a_send, a_recv, 0, to, to).start()

    def par_copy(step):
        return pltpu.make_async_remote_copy(
            src_ref=par_ref,
            dst_ref=parw.at[1 - step],
            send_sem=p_send.at[1 - step],
            recv_sem=p_recv.at[1 - step],
            device_id=dev(lax.rem(me + D + step, D)),
            device_id_type=MESH,
        )

    for fetch in fetches[3:]:
        fetch.wait()
    par_copy(1).start()
    par_copy(-1).start()
    recv[me] = send[me]
    parw[1] = par_ref[...]

    half_lanes = lax.broadcasted_iota(i32, (4, LANES), 1) < cap
    all_of(recv, a_send, a_recv, 0, D - 1).wait_recv()

    for t in range(tiles):
        at = slice(t * LANES, (t + 1) * LANES)
        if folds == 2:
            a, b = recv[2 * t], recv[2 * t + 1]
            flat[0:4, at] = jnp.where(half_lanes, a, pltpu.roll(b, cap, 1))
            flat[4:8, at] = jnp.where(half_lanes, pltpu.roll(a, cap, 1), b)
        else:
            total = recv[t * per]
            for g in range(1, per):
                total = total + pltpu.roll(recv[t * per + g], g * cap, 1)
            flat[:, at] = total
    arrived = split3_parts(flat[...])
    lane_hot = hot(rows_of((LANES, slots)) + 1.0 == flat[6:7, :])
    tile_row = flat[7:8, :]
    masked = [
        jnp.where(tile_row == float(t), part, 0.0)
        for t in range(node_tiles)
        for part in arrived
    ]
    placed = dot_t(jnp.concatenate(masked, axis=0).astype(bf16), lane_hot)
    unit = jnp.where(
        lax.broadcasted_iota(i32, (8, LANES), 0) < 3, 1.0 / softening, 1.0
    )
    placed_tiles = [joined(placed[24 * t : 24 * t + 24]) * unit for t in range(node_tiles)]
    last = placed_tiles[-1]
    for t in range(node_tiles - 1):
        mine[8 * t : 8 * t + 6, :] = placed_tiles[t][0:6]
        mine[8 * t + 6 : 8 * t + 8, :] = last[2 * t : 2 * t + 2]

    def halo(k, act):
        there = me - k if act == "wait_recv" else me + k

        @pl.when((there >= 0) & (there < D))
        def _():
            copy = pltpu.make_async_remote_copy(
                src_ref=mine,
                dst_ref=wide.at[reach - k],
                send_sem=h_send.at[reach - k],
                recv_sem=h_recv.at[reach - k],
                device_id=dev(there),
                device_id_type=MESH,
            )
            getattr(copy, act)()

    for k in sorted(range(1, reach + 1), key=lambda k: (abs(2 * k - reach), -k)):
        halo(k, "start")
        halo(-k, "start")

    wide[reach] = mine[...]
    for t in range(node_tiles):
        turned = jnp.transpose(placed_tiles[t])
        at = slice(t * LANES, (t + 1) * LANES)
        for c in range(3):
            spots[c, at, :] = jnp.broadcast_to(turned[:, c : c + 1], (LANES, LANES))

    par_copy(1).wait()
    par_copy(-1).wait()
    diagonal_of = (leaves, leaves)
    diagonal = lax.broadcasted_iota(i32, diagonal_of, 0) == lax.broadcasted_iota(
        i32, diagonal_of, 1
    )

    def column(row):
        return jnp.sum(jnp.where(diagonal, row.astype(f32), 0.0), axis=1, keepdims=True)

    wanted = column(lpar_ref[...] - (me - 1) * n_par)
    parts = []
    for c in range(3):
        total = jnp.zeros((leaves, LANES), f32)
        for j in range(3 * n_par):
            row = parw[j // n_par, c, j % n_par : j % n_par + 1, :]
            total = jnp.where(wanted == j, row, total)
        parts.append(total)
    wide_row = jnp.concatenate(parts, axis=1)
    high = wide_row.astype(bf16)
    low = (wide_row - high.astype(f32)).astype(bf16)
    both = jnp.concatenate([high, low], axis=0)
    octant = column(loct_ref[...])

    stage[3:4, :] = jnp.zeros((1, nodes), f32)
    for t in range(tiles):
        at = slice(t * LANES, (t + 1) * LANES)
        lane = jnp.maximum(flat[6:7, at] - 1.0, 0.0).astype(i32)
        lane_at[t] = jnp.broadcast_to(lane, (8, LANES))
        tile_at_slot[t] = jnp.broadcast_to(flat[7:8, at], (8, LANES))

    maps_copy.wait()
    trans[...] = jnp.zeros(trans.shape, f32)

    @pl.loop(0, maps_v.shape[0])
    def _(o):
        m = maps_v[o]
        m_high = m.astype(bf16)
        m_low = (m - m_high.astype(f32)).astype(bf16)
        first = dot_t(both, m_high)
        image = first[0:leaves] + (first[leaves : 2 * leaves] + dot_t(high, m_low))
        trans[...] = jnp.where(octant == jnp.asarray(o, i32).astype(f32), image, trans[...])

    for c in range(3):
        dens[c] = lloc_ref[c] + trans[:, c * LANES : (c + 1) * LANES]

    def pair_sums(targets, gaps_from, strengths, soft_by, sums):
        gap = [targets[c] - gaps_from[c] for c in range(3)]
        d2 = gap[0] * gap[0] + gap[1] * gap[1] + gap[2] * gap[2]
        soft = d2 + 1.0 if soft_by else d2
        inverse = lax.rsqrt(soft)
        weight = inverse * inverse * inverse
        along = gap[0] * strengths[0] + gap[1] * strengths[1] + gap[2] * strengths[2]
        near = inverse + weight if soft_by else inverse
        along = along * weight
        return [sums[c] + (near * strengths[c] + along * gap[c]) for c in range(3)]

    def leaf_rows(leaf):
        return pl.ds(pl.multiple_of(leaf * points, points), points)

    @pl.loop(0, leaves)
    def _(leaf):
        at = leaf_rows(leaf)
        targets = [spots[c, at, :] for c in range(3)]
        center = [jnp.sum(x, axis=0, keepdims=True) * (1.0 / points) for x in targets]
        spread = [
            jnp.max(jnp.abs(targets[c] - center[c]), axis=0, keepdims=True) for c in range(3)
        ]
        half = jnp.maximum(jnp.maximum(spread[0], spread[1]), spread[2])
        half = half + box_margin / softening
        points_at = [
            center[c] + shell_radius * half * shell_ref[c : c + 1, :] for c in range(3)
        ]
        density = [dens[c, pl.ds(leaf, 1), :] for c in range(3)]
        zero = jnp.zeros((points, LANES), f32)
        sums = pair_sums(targets, points_at, density, False, [zero, zero, zero])
        for c in range(3):
            acc[c, at, :] = sums[c]

    lane_group = lax.broadcasted_iota(i32, (8, LANES), 1) // points

    def spread_out(j):
        for t in range(node_tiles):
            if t < node_tiles - 1:
                tile = wide[j, 8 * t : 8 * t + 8, :]
            else:
                ends = [wide[j, 8 * i + 6 : 8 * i + 8, :] for i in range(node_tiles - 1)]
                tile = jnp.concatenate(ends + ends[0:1], axis=0)
            turned = [tile] + [pltpu.roll(tile, s * points, 1) for s in range(1, in_tile)]
            for i in range(in_tile):
                full = turned[(-i) % in_tile]
                for g in range(1, in_tile):
                    full = jnp.where(lane_group == g, turned[(g - i) % in_tile], full)
                rep[j * leaves + t * in_tile + i] = full

    spread_out(reach)
    together = reach

    @pl.loop(0, reach // together)
    def _(step):
        ks = [step * together + 1 + i for i in range(together)]
        for k in ks:
            halo(k, "wait_recv")
            halo(-k, "wait_recv")
        for k in ks:
            spread_out(reach - k)
            spread_out(reach + k)

    first_leaf = (me - reach) * leaves

    def table_row(leaf, n):
        row = near_ref[leaf, n] - first_leaf
        return jnp.minimum(jnp.maximum(row, 0), rep.shape[0] - 1)

    def near_field(leaf):
        at = leaf_rows(leaf)
        targets = [spots[c, at, :] for c in range(3)]
        sums = [acc[c, at, :] for c in range(3)]
        for base in range(0, near_count, in_tile):
            count = min(in_tile, near_count - base)
            source = rep[table_row(leaf, base)]
            for g in range(1, count):
                source = jnp.where(lane_group == g, rep[table_row(leaf, base + g)], source)
            if count < in_tile:
                row = lax.broadcasted_iota(i32, (8, LANES), 0)
                source = jnp.where((lane_group >= count) & (row >= 3), 0.0, source)
            sums = pair_sums(
                targets,
                [source[c : c + 1] for c in range(3)],
                [source[c + 3 : c + 4] for c in range(3)],
                True,
                sums,
            )
        for c in range(3):
            acc[c, at, :] = sums[c]

    def row_sums(t):
        at = pl.ds(pl.multiple_of(t * LANES, LANES), LANES)
        for row, c in ((0, 0), (1, 2), (2, 1)):
            speed = jnp.sum(jnp.transpose(acc[c, at, :]), axis=0, keepdims=True)
            stage[row : row + 1, at] = speed * (1.0 / (eight_pi * softening))

    @pl.loop(0, node_tiles)
    def _(t):
        row_sums(jnp.maximum(t - 1, 0))
        for i in range(in_tile):
            near_field(t * in_tile + i)

    row_sums(node_tiles - 1)
    pairs = [
        jnp.concatenate(
            [stage[0:4, t * LANES : (t + 1) * LANES] for t in range(p, p + 2)], axis=0
        )
        for p in range(0, node_tiles, 2)
    ]
    for t in range(tiles):
        at = slice(t * LANES, (t + 1) * LANES)
        lane, tile = lane_at[t], tile_at_slot[t]
        found = jnp.take_along_axis(pairs[0], lane, axis=1)
        for p in range(1, len(pairs)):
            more = jnp.take_along_axis(pairs[p], lane, axis=1)
            found = jnp.where(tile >= float(2 * p), more, found)
        even = tile - jnp.floor(tile * 0.5) * 2.0
        found = jnp.where(even[0:4] > 0.5, found[4:8], found[0:4])
        if folds == 2:
            turned = pltpu.roll(found, cap, 1)
            left = half_lanes[0:2]
            rsend[2 * t] = jnp.where(left, found[0:2], turned[2:4])
            rsend[2 * t + 1] = jnp.where(left, turned[0:2], found[2:4])
        else:
            for g in range(per):
                rsend[t * per + g] = pltpu.roll(found, (LANES - g * cap) % LANES, 1)

    @pl.loop(1, D)
    def _(k):
        to = partner(k)
        a2a(rsend, rrecv, r_send, r_recv, 0, to, to).start()

    rrecv[me] = rsend[me]

    all_of(recv, a_send, a_recv, 0, D - 1).wait_send()

    @pl.loop(1, reach + 1)
    def _(k):
        halo(k, "wait_send")
        halo(-k, "wait_send")

    back = 4 // folds
    ahead = jnp.concatenate([owner_of(slot_ref[...].astype(f32))] * folds, axis=1)
    ahead = ahead - rows_of((8, folds * nodes), back)

    all_of(rrecv, r_send, r_recv, 0, D - 1).wait_recv()

    got = jnp.concatenate([rrecv[o] for o in range(D)], axis=0)
    got_high = got.astype(bf16)
    got_low = (got - got_high.astype(f32)).astype(bf16)
    sides = [rank_hot[h] for h in range(folds)]
    found = dot_n(
        jnp.concatenate([got_high, got_low], axis=0),
        jnp.concatenate(sides, axis=1) if folds > 1 else sides[0],
    )
    total = jnp.zeros((8, folds * nodes), f32)
    for b in range(0, D * back, 8):
        both_rows = found[b : b + 8] + found[D * back + b : D * back + b + 8]
        total = jnp.where(ahead == float(b // back), both_rows, total)
    while total.shape[0] > back:
        middle = total.shape[0] // 2
        total = total[0:middle] + total[middle:]
    out_ref[0:back, :] = total[:, 0:nodes]
    if folds > 1:
        out_ref[back : 2 * back, :] = total[:, nodes:]

    all_of(rrecv, r_send, r_recv, 0, D - 1).wait_send()


def final(nodes_ref, ten_ref, blocks_v, out_ref):
    at_nodes = nodes_ref[...]
    fibers = blocks_v.shape[0]
    npf = at_nodes.shape[1] // fibers
    per_tile = LANES // npf
    left = lax.broadcasted_iota(i32, (1, LANES), 1) < npf
    for i in range(fibers):
        t, g = i // per_tile, i % per_tile
        lanes = slice(t * LANES, (t + 1) * LANES)
        x, z, y = (at_nodes[c : c + 1, lanes] for c in range(3))
        tension = ten_ref[0:1, lanes]

        def side(v, to):
            turn = ((to - g) * npf) % LANES
            return pltpu.roll(v, turn, 1) if turn else v

        first = jnp.where(left, side(x, 0), side(y, 1))
        second = jnp.where(left, side(z, 0), side(tension, 1))
        products = blocks_v[i, :, 0:LANES] * first + blocks_v[i, :, LANES : 2 * LANES] * second
        half = products.shape[0] // 2
        out_ref[i : i + 1, half:] = lane_sums(products[half:])[0:1]
        turned = jnp.transpose(products[0:half])
        out_ref[i : i + 1, 0:half] = jnp.sum(turned, axis=0, keepdims=True)


def send_form(cap):
    folds = 2 if LANES == 2 * cap else 1
    return folds, 8 // folds


def kernel(dims, count, *refs):
    given, held = refs[0:count], refs[count + 2 : 2 * count + 2]
    fetch_sem = refs[-1]
    fetches = [
        pltpu.make_async_copy(given[n], held[n], fetch_sem.at[n]) for n in range(count)
    ]
    body(dims, fetches, *held, *refs[count : count + 2], *refs[2 * count + 2 : -1])


def local(
    positions,
    forces,
    tension,
    node_slot,
    leaf_local,
    parent_local,
    l2l_maps,
    leaf_parent,
    leaf_octant,
    near_list,
    blocks,
):
    major, minor = lax.axis_size("aa"), lax.axis_size("ba")
    D = major * minor
    nodes = node_slot.shape[0]
    leaves, _, shell = leaf_local.shape
    reach = -(-NEAR_SPAN // leaves)
    cap = MOST * (nodes // D)
    slots = D * cap
    fibers, unknowns, _ = blocks.shape
    node_tiles = nodes // LANES
    _, rows_sent = send_form(cap)
    vmem = pl.BlockSpec(memory_space=pltpu.VMEM)
    anywhere = pl.BlockSpec(memory_space=pl.ANY)
    dma = pltpu.SemaphoreType.DMA
    operands = (
        node_slot.reshape(1, nodes),
        positions,
        forces,
        leaf_local.transpose(1, 0, 2),
        parent_local.transpose(1, 0, 2),
        leaf_parent.reshape(1, leaves),
        leaf_octant.reshape(1, leaves),
        near_list,
        surface(shell),
    )
    held = [
        (pltpu.SMEM if x is near_list else pltpu.VMEM)(x.shape, x.dtype) for x in operands
    ]
    at_nodes = pl.pallas_call(
        functools.partial(kernel, (major, minor, reach), len(operands)),
        out_shape=pltpu.VMEM((4, nodes), f32),
        in_specs=[anywhere] * (len(operands) + 1),
        out_specs=vmem,
        scratch_shapes=held
        + [
            pltpu.VMEM(l2l_maps.shape, f32),
            pltpu.VMEM((LANES // cap, LANES, nodes), bf16),
            pltpu.VMEM((8, nodes), f32),
            pltpu.VMEM((8, slots), f32),
            pltpu.VMEM((D, rows_sent, LANES), f32),
            pltpu.VMEM((D, rows_sent, LANES), f32),
            pltpu.VMEM((8 * (node_tiles - 1), LANES), f32),
            pltpu.VMEM((2 * reach + 1, 8 * (node_tiles - 1), LANES), f32),
            pltpu.VMEM(((2 * reach + 1) * leaves, 8, LANES), f32),
            pltpu.VMEM((3, nodes, LANES), f32),
            pltpu.VMEM((3, 3, parent_local.shape[0], shell), f32),
            pltpu.VMEM((leaves, 3 * shell), f32),
            pltpu.VMEM((3, leaves, shell), f32),
            pltpu.VMEM((3, nodes, LANES), f32),
            pltpu.VMEM((D, rows_sent // 2, LANES), f32),
            pltpu.VMEM((D, rows_sent // 2, LANES), f32),
            pltpu.VMEM((slots // LANES, 8, LANES), i32),
            pltpu.VMEM((slots // LANES, 8, LANES), f32),
            dma((1,)),
            dma((2,)),
            dma((2,)),
            dma((3,)),
            dma((3,)),
            dma((2 * reach + 1,)),
            dma((2 * reach + 1,)),
            dma((1,)),
            dma((1,)),
            dma((len(operands),)),
        ],
        compiler_params=pltpu.CompilerParams(
            collective_id=0, has_side_effects=True, vmem_limit_bytes=56 * 2**20
        ),
    )(*operands, l2l_maps)
    return pl.pallas_call(
        final,
        out_shape=jax.ShapeDtypeStruct((fibers, unknowns), f32),
        in_specs=[vmem, vmem, vmem],
        out_specs=vmem,
        compiler_params=pltpu.CompilerParams(vmem_limit_bytes=8 * 2**20),
    )(at_nodes, tension.reshape(1, nodes), blocks)


def solution(mesh):
    in_specs = (
        P(None, ("aa", "ba")),
        P(None, ("aa", "ba")),
        P(("aa", "ba")),
        P(("aa", "ba")),
        P(("aa", "ba"), None, None),
        P(("aa", "ba"), None, None),
        P(),
        P(("aa", "ba")),
        P(("aa", "ba")),
        P(("aa", "ba"), None),
        P(("aa", "ba"), None, None),
    )
    out_specs = P(("aa", "ba"), None)
    return jax.shard_map(local, mesh=mesh, in_specs=in_specs, out_specs=out_specs, check_vma=False)
```
